32 devices in a mesh: segment: 4 (over x, core), mp: 8 (over z, y).
Axes of the slice: x: 2, y: 2, z: 4, core: 2. Of those that a mesh axis runs over, the one named last changes fastest.
Arguments:
- frames_in: bfloat16 [1024, 1536], P('mp'), may hold values from -6 to 6
- section_weights: bfloat16 [4, 1536, 1536], P('segment', 'mp'), may hold values from -0.15625 to 0.15625
- conv_kernels: bfloat16 [4, 31, 1536], P('segment'), may hold values from -1 to 1
- valid_length: int32 [1], replicated, may hold values from 512 to 1024
- out_cotangent: bfloat16 [1024, 1536], P('mp'), may hold values from -6 to 6
Outputs:
- section_outputs: bfloat16 [4, 1024, 1536], P('segment', 'mp')
- input_grads: bfloat16 [4, 1024, 1536], P('segment', 'mp')
- kernel_grads: float32 [4, 31, 1536], P('segment', None, 'mp')
The draws below stay inside these ranges and needn't reach their ends.
All inputs are finite; a program needn't handle non-finite values.
Results may differ from the reference program's by a relative error of at most 0.012.
Values may be sent and summed in bfloat16 or wider, within the bound.
A program may use at most 128 MiB of HBM per device.

```python
import jax
import jax.numpy as jnp
from jax import lax

D = 1536
KW = 31
TOKENS = 1024
N_SEGMENT = 4


def steps_of(own_key, shape, split, low, high):
    gain, own = 1.0, jax.random.fold_in(own_key, 6)
    for position, shards_of in split:
        draws = jnp.exp(jax.random.uniform(jax.random.fold_in(own, position), (shards_of,), jnp.float32, low / len(split), high / len(split)))
        gain = gain * jnp.repeat(draws, shape[position] // shards_of).reshape([-1 if axis == position else 1 for axis in range(len(shape))])
    return gain


def scatter_about(key, dims, spread, limit, cuts=(), kind=jnp.bfloat16):
    entries = jax.random.normal(key, dims, jnp.float32) * spread
    if len(cuts) > 0:
        entries = steps_of(key, dims, cuts, -0.22, 0.18) * entries
    return jnp.clip(entries, min=-limit, max=limit).astype(kind)


def setup_inputs(seed: int = 0) -> dict:
    seeds = jax.random.split(jax.random.key(seed), 6)
    frames_in = scatter_about(seeds[0], (TOKENS, D), 1.0, 6.0, ((0, 8),))
    section_weights = scatter_about(seeds[1], (N_SEGMENT, D, D), D ** -0.5, 0.15625, ((0, 4), (1, 8)))
    conv_kernels = scatter_about(seeds[2], (N_SEGMENT, KW, D), KW ** -0.5, 1.0, ((0, 4),))
    valid_length = jax.random.randint(seeds[3], (1,), TOKENS // 2, TOKENS + 1).astype(jnp.int32)
    out_cotangent = scatter_about(seeds[4], (TOKENS, D), 1.0, 6.0, ((0, 8),))
    return {"frames_in": frames_in, "section_weights": section_weights, "conv_kernels": conv_kernels, "valid_length": valid_length, "out_cotangent": out_cotangent}


EPSILON = 1e-05

def normalize(values):
    center = values - lax.optimization_barrier(jnp.mean(values, axis=-1, keepdims=True))
    inverse = lax.rsqrt(lax.optimization_barrier(jnp.mean(center * center, axis=-1, keepdims=True)) + EPSILON)
    return (center * inverse, inverse)

def tap_sum(kernel32, padded, length, forward):
    tap_count = kernel32.shape[0]
    running = jnp.zeros((length, kernel32.shape[1]), jnp.float32)
    for tap_index in range(tap_count):
        offset = tap_index if forward else tap_count - 1 - tap_index
        running = running + kernel32[tap_index] * padded[offset:offset + length].astype(jnp.float32)
    return running

def tap_grads(grad32, padded, length):
    rows_list = []
    for tap_index in range(KW):
        rows_list.append(lax.optimization_barrier(jnp.sum(grad32 * padded[tap_index:tap_index + length].astype(jnp.float32), axis=0)))
    return jnp.stack(rows_list)

def reference(frames_in, section_weights, conv_kernels, valid_length, out_cotangent):
    half_width = KW // 2
    valid_mask = (jnp.arange(TOKENS, dtype=jnp.int32) < valid_length[0]).astype(jnp.float32)[:, None]
    current = frames_in
    stored = []
    outputs = []
    for section in range(N_SEGMENT):
        kernel32 = conv_kernels[section].astype(jnp.float32)
        normed, inverse = normalize(current.astype(jnp.float32))
        masked = (normed * valid_mask).astype(jnp.bfloat16)
        padded = jnp.pad(masked, ((half_width, half_width), (0, 0)))
        conv_out = tap_sum(kernel32, padded, TOKENS, True)
        activated = (conv_out * jax.nn.sigmoid(conv_out)).astype(jnp.bfloat16)
        product = jnp.dot(activated, section_weights[section], preferred_element_type=jnp.float32)
        current = (current.astype(jnp.float32) + product).astype(jnp.bfloat16)
        stored.append((normed, inverse, padded, conv_out))
        outputs.append(current)
    upstream = out_cotangent
    input_list = [None] * N_SEGMENT
    kernel_list = [None] * N_SEGMENT
    for section in reversed(range(N_SEGMENT)):
        normed, inverse, padded, conv_out = stored[section]
        kernel32 = conv_kernels[section].astype(jnp.float32)
        grad_swish = lax.dot_general(upstream, section_weights[section], (((1,), (1,)), ((), ())), preferred_element_type=jnp.float32)
        gate_value = jax.nn.sigmoid(conv_out)
        grad_conv = (grad_swish * gate_value * (1.0 + conv_out * (1.0 - gate_value))).astype(jnp.bfloat16)
        grad_padded = jnp.pad(grad_conv, ((half_width, half_width), (0, 0)))
        grad_masked = tap_sum(kernel32, grad_padded, TOKENS, False) * valid_mask
        grad_input = inverse * (grad_masked - lax.optimization_barrier(jnp.mean(grad_masked, axis=-1, keepdims=True)) - normed * lax.optimization_barrier(jnp.mean(grad_masked * normed, axis=-1, keepdims=True)))
        upstream = (upstream.astype(jnp.float32) + grad_input).astype(jnp.bfloat16)
        input_list[section] = upstream
        kernel_list[section] = tap_grads(grad_conv.astype(jnp.float32), padded, TOKENS) * TOKENS ** (-0.5)
    return (jnp.stack(outputs), jnp.stack(input_list), jnp.stack(kernel_list))
```

```python
import functools

import jax
import jax.numpy as jnp
from jax import lax
from jax.experimental import pallas as pl
from jax.experimental.pallas import tpu as pltpu
from jax.sharding import PartitionSpec as P

EPSILON = 1e-05
PAD = 16
LANES = 128
ROWS = 16
WIDE = 256
MESH = pl.DeviceIdType.MESH
BF = jnp.bfloat16
F32 = jnp.float32


def cascade(
    x_ref, w_ref, k_ref, vl_ref, cot_ref,
    out_ref, gin_ref, kg_ref,
    cur, up, norm, inv, pm, pg, act, slope, gs,
    halo_send, halo_recv, in_send, in_recv, up_send, up_recv,
):
    frames, width = x_ref.shape
    taps = k_ref.shape[0]
    seg, mp = lax.axis_index("segment"), lax.axis_index("mp")
    n_seg, n_mp = lax.axis_size("segment"), lax.axis_size("mp")
    chunks = width // LANES
    blocks = frames // ROWS
    tiles = width // WIDE

    barrier = pltpu.get_barrier_semaphore()
    for axis, index, count in (("segment", seg, n_seg), ("mp", mp, n_mp)):
        for by in (1, count - 1):
            pl.semaphore_signal(
                barrier, inc=1, device_id={axis: lax.rem(index + by, count)}, device_id_type=MESH
            )
    pl.semaphore_wait(barrier, 4)

    def halo_copy(pad_ref, first, to_right):
        rows_from = pl.ds(frames, PAD) if to_right else pl.ds(PAD, PAD)
        rows_to = pl.ds(0, PAD) if to_right else pl.ds(frames + PAD, PAD)
        target = lax.rem(mp + (1 if to_right else n_mp - 1), n_mp)
        slot = first + (0 if to_right else 1)
        return pltpu.make_async_remote_copy(
            src_ref=pad_ref.at[rows_from], dst_ref=pad_ref.at[rows_to],
            send_sem=halo_send.at[slot], recv_sem=halo_recv.at[slot],
            device_id={"mp": target}, device_id_type=MESH,
        )

    def halo_start(pad_ref, first):
        @pl.when(mp < n_mp - 1)
        def _():
            halo_copy(pad_ref, first, True).start()

        @pl.when(mp > 0)
        def _():
            halo_copy(pad_ref, first, False).start()

    def halo_wait(pad_ref, first):
        @pl.when(mp > 0)
        def _():
            halo_copy(pad_ref, first, True).wait_recv()

        @pl.when(mp < n_mp - 1)
        def _():
            halo_copy(pad_ref, first, False).wait_recv()

    def halo_sent(pad_ref, first):
        @pl.when(mp < n_mp - 1)
        def _():
            halo_copy(pad_ref, first, True).wait_send()

        @pl.when(mp > 0)
        def _():
            halo_copy(pad_ref, first, False).wait_send()

    def halo_clear(pad_ref):
        @pl.when(mp == 0)
        def _():
            pad_ref[0:PAD, :] = jnp.zeros((PAD, width), BF)

        @pl.when(mp == n_mp - 1)
        def _():
            pad_ref[frames + PAD : frames + 2 * PAD, :] = jnp.zeros((PAD, width), BF)

    def in_copy(tile):
        columns = pl.ds(tile * WIDE, WIDE)
        return pltpu.make_async_remote_copy(
            src_ref=out_ref.at[:, columns], dst_ref=cur.at[:, columns],
            send_sem=in_send.at[tile], recv_sem=in_recv.at[tile],
            device_id={"segment": lax.rem(seg + 1, n_seg)}, device_id_type=MESH,
        )

    def up_copy(block):
        rows = pl.ds(block * ROWS, ROWS)
        return pltpu.make_async_remote_copy(
            src_ref=gin_ref.at[rows], dst_ref=up.at[rows],
            send_sem=up_send.at[block], recv_sem=up_recv.at[block],
            device_id={"segment": lax.rem(seg + n_seg - 1, n_seg)}, device_id_type=MESH,
        )

    def mask_rows(start, count):
        position = mp * frames + start + lax.broadcasted_iota(jnp.int32, (count, LANES), 0)
        return (position < vl_ref[0]).astype(F32)

    def back_product():
        for tile in range(tiles):
            columns = slice(tile * WIDE, (tile + 1) * WIDE)
            gs[:, columns] = lax.dot_general(
                up[...], w_ref[columns, :], (((1,), (1,)), ((), ())), preferred_element_type=F32
            )

    halo_clear(pm)
    halo_clear(pg)

    @pl.when(seg == n_seg - 1)
    def _():
        up[...] = cot_ref[...]
        back_product()

    @pl.when(seg == 0)
    def _():
        cur[...] = x_ref[...]

    @pl.when(seg > 0)
    def _():
        for tile in range(tiles):
            in_copy(tile).wait_recv()

    def norm_rows(block):
        start = pl.multiple_of(block * ROWS, ROWS)
        rows = pl.ds(start, ROWS)
        values = cur[rows, :].astype(F32)
        center = values - jnp.mean(values, axis=-1, keepdims=True)
        inverse = lax.rsqrt(jnp.mean(center * center, axis=-1, keepdims=True) + EPSILON)
        normed = center * inverse
        norm[rows, :] = normed
        inv[rows, :] = jnp.broadcast_to(inverse, (ROWS, LANES))
        pm[pl.ds(pl.multiple_of(PAD + start, ROWS), ROWS), :] = (
            normed * mask_rows(start, ROWS)[:, :1]
        ).astype(BF)

    norm_rows(0)
    norm_rows(blocks - 1)
    halo_start(pm, 0)

    @pl.loop(1, blocks - 1)
    def _(block):
        norm_rows(block)

    halo_wait(pm, 0)

    def shifted(padded):
        total = padded.shape[0]
        return [padded if r == 0 else pltpu.roll(padded, total - r, 0) for r in range(8)]

    def tap_sum(padded, columns, forward):
        total = padded.shape[0]
        running = jnp.zeros((frames, LANES), F32)
        for r in range(8):
            moved = padded if r == 0 else pltpu.roll(padded, total - r, 0)
            for base in range(0, 2 * PAD, 8):
                offset = base + r
                if 1 <= offset <= taps:
                    tap = offset - 1 if forward else taps - offset
                    running = running + k_ref[tap : tap + 1, columns] * moved[base : base + frames]
        return running

    @pl.loop(0, chunks)
    def _(chunk):
        columns = pl.ds(pl.multiple_of(chunk * LANES, LANES), LANES)
        conv = tap_sum(pm[:, columns].astype(F32), columns, True)
        gate = jax.nn.sigmoid(conv)
        act[:, columns] = (conv * gate).astype(BF)
        slope[:, columns] = gate * (1.0 + conv * (1.0 - gate))

    for tile in range(tiles):
        columns = slice(tile * WIDE, (tile + 1) * WIDE)
        product = jnp.dot(act[...], w_ref[:, columns], preferred_element_type=F32)
        out_ref[:, columns] = (cur[:, columns].astype(F32) + product).astype(BF)

        @pl.when(seg < n_seg - 1)
        def _():
            in_copy(tile).start()

    @pl.when(seg < n_seg - 1)
    def _():
        for block in range(blocks):
            up_copy(block).wait_recv()
        back_product()

    def grad_rows(block):
        start = pl.multiple_of(block * ROWS, ROWS)
        rows = pl.ds(start, ROWS)
        pg[pl.ds(pl.multiple_of(PAD + start, ROWS), ROWS), :] = (
            gs[rows, :] * slope[rows, :]
        ).astype(BF)

    grad_rows(0)
    grad_rows(blocks - 1)
    halo_start(pg, 2)

    @pl.loop(1, blocks - 1)
    def _(block):
        grad_rows(block)

    halo_wait(pg, 2)

    @pl.loop(0, chunks)
    def _(chunk):
        columns = pl.ds(pl.multiple_of(chunk * LANES, LANES), LANES)
        gs[:, columns] = tap_sum(pg[:, columns].astype(F32), columns, False) * mask_rows(0, frames)

    @pl.loop(0, blocks)
    def _(block):
        rows = pl.ds(pl.multiple_of(block * ROWS, ROWS), ROWS)
        masked = gs[rows, :]
        normed = norm[rows, :]
        first = jnp.mean(masked, axis=-1, keepdims=True)
        second = jnp.mean(masked * normed, axis=-1, keepdims=True)
        grad = inv[rows, :][:, :1] * (masked - first - normed * second)
        gin_ref[rows, :] = (up[rows, :].astype(F32) + grad).astype(BF)

        @pl.when(seg > 0)
        def _():
            up_copy(block).start()

    @pl.loop(0, chunks)
    def _(chunk):
        columns = pl.ds(pl.multiple_of(chunk * LANES, LANES), LANES)
        padded = pm[:, columns].astype(F32)
        grad = pg[PAD : PAD + frames, columns].astype(F32)
        total = padded.shape[0]
        for r in range(8):
            moved = padded if r == 0 else pltpu.roll(padded, total - r, 0)
            for base in range(0, 2 * PAD, 8):
                tap = base + r - 1
                if 0 <= tap < taps:
                    kg_ref[tap : tap + 1, columns] = jnp.sum(
                        grad * moved[base : base + frames], axis=0, keepdims=True
                    )

    halo_sent(pm, 0)
    halo_sent(pg, 2)

    @pl.when(seg < n_seg - 1)
    def _():
        for tile in range(tiles):
            in_copy(tile).wait_send()

    @pl.when(seg > 0)
    def _():
        for block in range(blocks):
            up_copy(block).wait_send()


def on_device(frames_in, section_weights, conv_kernels, valid_length, out_cotangent):
    frames, width = frames_in.shape
    taps = conv_kernels.shape[1]
    weight = lax.all_gather(section_weights[0], "mp", axis=0, tiled=True)
    vmem = pl.BlockSpec(memory_space=pltpu.VMEM)
    smem = pl.BlockSpec(memory_space=pltpu.SMEM)
    padded = (frames + 2 * PAD, width)
    dma = pltpu.SemaphoreType.DMA
    out, gin, part = pl.pallas_call(
        cascade,
        out_shape=(
            jax.ShapeDtypeStruct((frames, width), BF),
            jax.ShapeDtypeStruct((frames, width), BF),
            jax.ShapeDtypeStruct((taps, width), F32),
        ),
        in_specs=[vmem, vmem, vmem, smem, vmem],
        out_specs=(vmem, vmem, vmem),
        scratch_shapes=[
            pltpu.VMEM((frames, width), BF),
            pltpu.VMEM((frames, width), BF),
            pltpu.VMEM((frames, width), F32),
            pltpu.VMEM((frames, LANES), F32),
            pltpu.VMEM(padded, BF),
            pltpu.VMEM(padded, BF),
            pltpu.VMEM((frames, width), BF),
            pltpu.VMEM((frames, width), F32),
            pltpu.VMEM((frames, width), F32),
            dma((4,)), dma((4,)),
            dma((width // WIDE,)), dma((width // WIDE,)),
            dma((frames // ROWS,)), dma((frames // ROWS,)),
        ],
        compiler_params=pltpu.CompilerParams(
            collective_id=0, has_side_effects=True, vmem_limit_bytes=48 * 2**20
        ),
    )(frames_in, weight, conv_kernels[0].astype(F32), valid_length, out_cotangent)
    grad = lax.psum_scatter(part, "mp", scatter_dimension=1, tiled=True)
    grad = grad * (frames * lax.axis_size("mp")) ** (-0.5)
    return (out[None], gin[None], grad[None])


def solution(mesh):
    in_specs = (
        P("mp", None),
        P("segment", "mp", None),
        P("segment", None, None),
        P(),
        P("mp", None),
    )
    out_specs = (P("segment", "mp", None), P("segment", "mp", None), P("segment", None, "mp"))
    return jax.shard_map(
        on_device, mesh=mesh, in_specs=in_specs, out_specs=out_specs, check_vma=False
    )
```

```python
import functools

import jax
import jax.numpy as jnp
from jax import lax
from jax.experimental import pallas as pl
from jax.experimental.pallas import tpu as pltpu
from jax.sharding import PartitionSpec as P

EPSILON = 1e-05
PAD = 16
LANES = 128
ROWS = 16
WIDE = 256
MESH = pl.DeviceIdType.MESH
BF = jnp.bfloat16
F32 = jnp.float32


def cascade(
    relay, x_any, w_any, k_bf, vl_ref, cot_any,
    out_whole, gin_whole, kg_out,
    cur, up, norm, inv, pm, pg, act, slope, gs, w_ref, k_ref, kg_ref, kg_land,
    halo_send, halo_recv, in_send, in_recv, up_send, up_recv,
    local_sem, w_send, w_recv, kg_send, kg_recv, turn_sem,
):
    out_ref, gin_ref = out_whole.at[0], gin_whole.at[0]
    frames, width = x_any.shape
    taps = k_ref.shape[0]
    seg, mp = lax.axis_index("segment"), lax.axis_index("mp")
    n_seg, n_mp = lax.axis_size("segment"), lax.axis_size("mp")
    chunks = width // LANES
    blocks = frames // ROWS
    tiles = width // WIDE

    barrier = pltpu.get_barrier_semaphore()
    steps_mp = range(1, n_mp) if relay else (1, n_mp - 1)
    for axis, index, count, steps in (
        ("segment", seg, n_seg, (1, n_seg - 1)), ("mp", mp, n_mp, steps_mp)
    ):
        for by in steps:
            pl.semaphore_signal(
                barrier, inc=1, device_id={axis: lax.rem(index + by, count)}, device_id_type=MESH
            )
    own = width // n_mp
    w_rows = pl.ds(pl.multiple_of(mp * own, own), own) if relay else pl.ds(0, width)
    w_copy = pltpu.make_async_copy(w_any, w_ref.at[w_rows], local_sem.at[0])
    x_copy = pltpu.make_async_copy(x_any, cur, local_sem.at[1])
    cot_copy = pltpu.make_async_copy(cot_any, up, local_sem.at[2])
    w_copy.start()

    @pl.when(seg == 0)
    def _():
        x_copy.start()

    @pl.when(seg == n_seg - 1)
    def _():
        cot_copy.start()

    pl.semaphore_wait(barrier, 2 + len(steps_mp))

    row, column = lax.div(mp, 2), lax.rem(mp, 2)
    n_row = n_mp // 2

    def block_copy(block, way):
        rows = pl.ds(pl.multiple_of(block * own, own), own)
        target = (mp + 2, mp - 2, mp + 1 - 2 * column)[way]
        return pltpu.make_async_remote_copy(
            src_ref=w_ref.at[rows], dst_ref=w_ref.at[rows],
            send_sem=w_send.at[way, block], recv_sem=w_recv.at[block],
            device_id={"mp": target}, device_id_type=MESH,
        )

    def each_block(distance, act_on, arrive):
        if distance == 0:
            pl.when(row < n_row - 1)(lambda: act_on(mp, 0))
            pl.when(row > 0)(lambda: act_on(mp, 1))
            act_on(mp, 2)
            return
        low, high = mp - 2 * distance, mp + 2 * distance

        @pl.when(row >= distance)
        def _():
            arrive(low)
            pl.when(row < n_row - 1)(lambda: act_on(low, 0))
            act_on(low, 2)

        @pl.when(row + distance < n_row)
        def _():
            arrive(high)
            pl.when(row > 0)(lambda: act_on(high, 1))
            act_on(high, 2)

    def pass_on(distance):
        each_block(
            distance,
            lambda block, way: block_copy(block, way).start(),
            lambda block: block_copy(block, 0).wait_recv(),
        )

    def passed():
        for distance in range(n_row):
            each_block(
                distance,
                lambda block, way: block_copy(block, way).wait_send(),
                lambda block: None,
            )

    def gather_rest(first):
        if relay:
            for distance in range(first, n_row):
                pass_on(distance)
            for index in range(n_row):
                block_copy(index * 2 + 1 - column, 2).wait_recv()

    def kg_copy(target, sender):
        start = 384 * lax.div(target, 2) + 128 * lax.rem(target, 2)
        window = pl.ds(pl.multiple_of(start, LANES), 2 * LANES)
        return pltpu.make_async_remote_copy(
            src_ref=kg_ref.at[:, window], dst_ref=kg_land.at[sender],
            send_sem=kg_send.at[target], recv_sem=kg_recv.at[sender],
            device_id={"mp": target}, device_id_type=MESH,
        )

    w_copy.wait()
    if relay:

        @pl.when(seg != 1)
        def _():
            pass_on(0)

    k_ref[...] = k_bf[...].astype(F32)
    kg_ref[...] = jnp.zeros(kg_ref.shape, F32)

    def halo_copy(pad_ref, first, to_right):
        rows_from = pl.ds(frames, PAD) if to_right else pl.ds(PAD, PAD)
        rows_to = pl.ds(0, PAD) if to_right else pl.ds(frames + PAD, PAD)
        target = lax.rem(mp + (1 if to_right else n_mp - 1), n_mp)
        slot = first + (0 if to_right else 1)
        return pltpu.make_async_remote_copy(
            src_ref=pad_ref.at[rows_from], dst_ref=pad_ref.at[rows_to],
            send_sem=halo_send.at[slot], recv_sem=halo_recv.at[slot],
            device_id={"mp": target}, device_id_type=MESH,
        )

    def halo_start(pad_ref, first):
        @pl.when(mp < n_mp - 1)
        def _():
            halo_copy(pad_ref, first, True).start()

        @pl.when(mp > 0)
        def _():
            halo_copy(pad_ref, first, False).start()

    def halo_wait(pad_ref, first):
        @pl.when(mp > 0)
        def _():
            halo_copy(pad_ref, first, True).wait_recv()

        @pl.when(mp < n_mp - 1)
        def _():
            halo_copy(pad_ref, first, False).wait_recv()

    def halo_sent(pad_ref, first):
        @pl.when(mp < n_mp - 1)
        def _():
            halo_copy(pad_ref, first, True).wait_send()

        @pl.when(mp > 0)
        def _():
            halo_copy(pad_ref, first, False).wait_send()

    def halo_clear(pad_ref):
        @pl.when(mp == 0)
        def _():
            pad_ref[0:PAD, :] = jnp.zeros((PAD, width), BF)

        @pl.when(mp == n_mp - 1)
        def _():
            pad_ref[frames + PAD : frames + 2 * PAD, :] = jnp.zeros((PAD, width), BF)

    def in_copy(tile):
        columns = pl.ds(tile * WIDE, WIDE)
        return pltpu.make_async_remote_copy(
            src_ref=out_ref.at[:, columns], dst_ref=cur.at[:, columns],
            send_sem=in_send.at[tile], recv_sem=in_recv.at[tile],
            device_id={"segment": lax.rem(seg + 1, n_seg)}, device_id_type=MESH,
        )

    def up_copy(block):
        rows = pl.ds(block * ROWS, ROWS)
        return pltpu.make_async_remote_copy(
            src_ref=gin_ref.at[rows], dst_ref=up.at[rows],
            send_sem=up_send.at[block], recv_sem=up_recv.at[block],
            device_id={"segment": lax.rem(seg + n_seg - 1, n_seg)}, device_id_type=MESH,
        )

    def mask_rows(start, count):
        position = mp * frames + start + lax.broadcasted_iota(jnp.int32, (count, LANES), 0)
        return (position < vl_ref[0]).astype(F32)

    def back_product():
        for tile in range(tiles):
            columns = slice(tile * WIDE, (tile + 1) * WIDE)
            gs[:, columns] = lax.dot_general(
                up[...], w_ref[columns, :], (((1,), (1,)), ((), ())), preferred_element_type=F32
            )

    halo_clear(pm)
    halo_clear(pg)

    @pl.when(seg == n_seg - 1)
    def _():
        gather_rest(1)
        cot_copy.wait()
        back_product()

    @pl.when(seg == 0)
    def _():
        x_copy.wait()

    @pl.when(seg == 1)
    def _():
        if relay:
            pl.semaphore_wait(turn_sem, 1)
        gather_rest(0)

    @pl.when((seg > 1) & (seg < n_seg - 1))
    def _():
        gather_rest(1)

    @pl.when(seg > 0)
    def _():
        for tile in range(tiles):
            in_copy(tile).wait_recv()

    def norm_rows(block):
        start = pl.multiple_of(block * ROWS, ROWS)
        rows = pl.ds(start, ROWS)
        values = cur[rows, :].astype(F32)
        center = values - jnp.mean(values, axis=-1, keepdims=True)
        inverse = lax.rsqrt(jnp.mean(center * center, axis=-1, keepdims=True) + EPSILON)
        normed = center * inverse
        norm[rows, :] = normed
        inv[rows, :] = jnp.broadcast_to(inverse, (ROWS, LANES))
        pm[pl.ds(pl.multiple_of(PAD + start, ROWS), ROWS), :] = (
            normed * mask_rows(start, ROWS)[:, :1]
        ).astype(BF)

    norm_rows(0)
    norm_rows(blocks - 1)
    halo_start(pm, 0)

    @pl.loop(1, blocks - 1)
    def _(block):
        norm_rows(block)

    if relay:

        @pl.when(seg == 0)
        def _():
            pass_on(1)

    halo_wait(pm, 0)

    def shifted(padded):
        total = padded.shape[0]
        return [padded if r == 0 else pltpu.roll(padded, total - r, 0) for r in range(8)]

    def tap_sum(padded, columns, forward):
        total = padded.shape[0]
        running = jnp.zeros((frames, LANES), F32)
        for r in range(8):
            moved = padded if r == 0 else pltpu.roll(padded, total - r, 0)
            for base in range(0, 2 * PAD, 8):
                offset = base + r
                if 1 <= offset <= taps:
                    tap = offset - 1 if forward else taps - offset
                    running = running + k_ref[tap : tap + 1, columns] * moved[base : base + frames]
        return running

    @pl.loop(0, chunks)
    def _(chunk):
        columns = pl.ds(pl.multiple_of(chunk * LANES, LANES), LANES)
        conv = tap_sum(pm[:, columns].astype(F32), columns, True)
        gate = jax.nn.sigmoid(conv)
        act[:, columns] = (conv * gate).astype(BF)
        slope[:, columns] = gate * (1.0 + conv * (1.0 - gate))

    @pl.when(seg == 0)
    def _():
        gather_rest(2)
        if relay:
            pl.semaphore_signal(
                turn_sem, inc=1, device_id={"segment": seg + 1}, device_id_type=MESH
            )

    for tile in range(tiles):
        columns = slice(tile * WIDE, (tile + 1) * WIDE)
        product = jnp.dot(act[...], w_ref[:, columns], preferred_element_type=F32)
        out_ref[:, columns] = (cur[:, columns].astype(F32) + product).astype(BF)

        @pl.when(seg < n_seg - 1)
        def _():
            in_copy(tile).start()

    @pl.when(seg < n_seg - 1)
    def _():
        for block in range(blocks):
            up_copy(block).wait_recv()
        back_product()

    def grad_rows(block):
        start = pl.multiple_of(block * ROWS, ROWS)
        rows = pl.ds(start, ROWS)
        pg[pl.ds(pl.multiple_of(PAD + start, ROWS), ROWS), :] = (
            gs[rows, :] * slope[rows, :]
        ).astype(BF)

    grad_rows(0)
    grad_rows(blocks - 1)
    halo_start(pg, 2)

    @pl.loop(1, blocks - 1)
    def _(block):
        grad_rows(block)

    kg_start = 384 * row + 128 * column
    kg_window = pl.ds(pl.multiple_of(kg_start, LANES), 2 * LANES)

    def tap_grads():
        @pl.loop(0, chunks)
        def _(chunk):
            columns = pl.ds(pl.multiple_of(chunk * LANES, LANES), LANES)
            padded = pm[:, columns].astype(F32)
            grad = pg[PAD : PAD + frames, columns].astype(F32)
            total = padded.shape[0]
            for r in range(8):
                moved = padded if r == 0 else pltpu.roll(padded, total - r, 0)
                for base in range(0, 2 * PAD, 8):
                    tap = base + r - 1
                    if 0 <= tap < taps:
                        kg_ref[tap : tap + 1, columns] = jnp.sum(
                            grad * moved[base : base + frames], axis=0, keepdims=True
                        )

        if relay:
            for by in range(1, n_mp):
                kg_copy(lax.rem(mp + by, n_mp), mp).start()

    @pl.when(seg == 0)
    def _():
        tap_grads()

    halo_wait(pg, 2)

    @pl.loop(0, chunks)
    def _(chunk):
        columns = pl.ds(pl.multiple_of(chunk * LANES, LANES), LANES)
        gs[:, columns] = tap_sum(pg[:, columns].astype(F32), columns, False) * mask_rows(0, frames)

    @pl.loop(0, blocks)
    def _(block):
        rows = pl.ds(pl.multiple_of(block * ROWS, ROWS), ROWS)
        masked = gs[rows, :]
        normed = norm[rows, :]
        first = jnp.mean(masked, axis=-1, keepdims=True)
        second = jnp.mean(masked * normed, axis=-1, keepdims=True)
        grad = inv[rows, :][:, :1] * (masked - first - normed * second)
        gin_ref[rows, :] = (up[rows, :].astype(F32) + grad).astype(BF)

        @pl.when(seg > 0)
        def _():
            up_copy(block).start()

    @pl.when(seg > 0)
    def _():
        tap_grads()

    if relay:
        total = kg_ref[:, kg_window]
        for by in range(1, n_mp):
            sender = lax.rem(mp + n_mp - by, n_mp)
            kg_copy(mp, sender).wait_recv()
            total = total + kg_land[sender]
        scale = (frames * n_mp) ** (-0.5)
        even, odd = total[:taps, :own], total[:taps, 2 * LANES - own :]
        kg_out[0] = jnp.where(column == 0, even, odd) * scale
        for by in range(1, n_mp):
            kg_copy(lax.rem(mp + by, n_mp), mp).wait_send()
        passed()
    else:
        kg_out[0] = kg_ref[:taps, :]

    halo_sent(pm, 0)
    halo_sent(pg, 2)

    @pl.when(seg < n_seg - 1)
    def _():
        for tile in range(tiles):
            in_copy(tile).wait_send()

    @pl.when(seg > 0)
    def _():
        for block in range(blocks):
            up_copy(block).wait_send()


def on_device(frames_in, section_weights, conv_kernels, valid_length, out_cotangent):
    frames, width = frames_in.shape
    taps = conv_kernels.shape[1]
    n_mp = lax.axis_size("mp")
    own = width // n_mp
    relay = own == 192 and n_mp == 8
    weight = section_weights[0]
    if not relay:
        weight = lax.all_gather(weight, "mp", axis=0, tiled=True)
    vmem = pl.BlockSpec(memory_space=pltpu.VMEM)
    smem = pl.BlockSpec(memory_space=pltpu.SMEM)
    whole = pl.BlockSpec(memory_space=pl.ANY)
    padded = (frames + 2 * PAD, width)
    tap_rows = -(-taps // 8) * 8
    dma = pltpu.SemaphoreType.DMA
    out, gin, grad = pl.pallas_call(
        functools.partial(cascade, relay),
        out_shape=(
            jax.ShapeDtypeStruct((1, frames, width), BF),
            jax.ShapeDtypeStruct((1, frames, width), BF),
            jax.ShapeDtypeStruct((1, taps, own if relay else width), F32),
        ),
        in_specs=[whole, whole, vmem, smem, whole],
        out_specs=(vmem, vmem, vmem),
        scratch_shapes=[
            pltpu.VMEM((frames, width), BF),
            pltpu.VMEM((frames, width), BF),
            pltpu.VMEM((frames, width), F32),
            pltpu.VMEM((frames, LANES), F32),
            pltpu.VMEM(padded, BF),
            pltpu.VMEM(padded, BF),
            pltpu.VMEM((frames, width), BF),
            pltpu.VMEM((frames, width), F32),
            pltpu.VMEM((frames, width), F32),
            pltpu.VMEM((width, width), BF),
            pltpu.VMEM((taps, width), F32),
            pltpu.VMEM((tap_rows, width), F32),
            pltpu.VMEM((n_mp if relay else 1, tap_rows, 2 * LANES), F32),
            dma((4,)), dma((4,)),
            dma((width // WIDE,)), dma((width // WIDE,)),
            dma((frames // ROWS,)), dma((frames // ROWS,)),
            dma((3,)),
            dma((3, n_mp)), dma((n_mp,)), dma((n_mp,)), dma((n_mp,)),
            pltpu.SemaphoreType.REGULAR,
        ],
        compiler_params=pltpu.CompilerParams(
            collective_id=0, has_side_effects=True, vmem_limit_bytes=48 * 2**20
        ),
    )(frames_in, weight, conv_kernels[0], valid_length, out_cotangent)
    if not relay:
        grad = lax.psum_scatter(grad, "mp", scatter_dimension=2, tiled=True)
        grad = grad * (frames * n_mp) ** (-0.5)
    return (out, gin, grad)


def solution(mesh):
    in_specs = (
        P("mp", None),
        P("segment", "mp", None),
        P("segment", None, None),
        P(),
        P("mp", None),
    )
    out_specs = (P("segment", "mp", None), P("segment", "mp", None), P("segment", None, "mp"))
    return jax.shard_map(
        on_device, mesh=mesh, in_specs=in_specs, out_specs=out_specs, check_vma=False
    )
```

```python
import functools

import jax
import jax.numpy as jnp
from jax import lax
from jax.experimental import pallas as pl
from jax.experimental.pallas import tpu as pltpu
from jax.sharding import PartitionSpec as P

EPSILON = 1e-05
PAD = 16
LANES = 128
ROWS = 16
WIDE = 256
MESH = pl.DeviceIdType.MESH
BF = jnp.bfloat16
F32 = jnp.float32


def cascade(
    relay, x_any, w_any, k_any, vl_ref, cot_any,
    out_whole, gin_whole, kg_out,
    cur, up, norm, inv, pm, pg, act, slope, gs, w_ref, k_bf, k_ref, kg_ref, kg_land,
    halo_send, halo_recv, in_send, in_recv, up_send, up_recv,
    local_sem, w_send, w_recv, kg_send, kg_recv, turn_sem,
):
    out_ref, gin_ref = out_whole.at[0], gin_whole.at[0]
    frames, width = x_any.shape
    taps = k_ref.shape[0]
    seg, mp = lax.axis_index("segment"), lax.axis_index("mp")
    n_seg, n_mp = lax.axis_size("segment"), lax.axis_size("mp")
    chunks = width // LANES
    blocks = frames // ROWS
    tiles = width // WIDE

    barrier = pltpu.get_barrier_semaphore()
    steps_mp = range(1, n_mp) if relay else (1, n_mp - 1)
    for axis, index, count, steps in (
        ("segment", seg, n_seg, (1, n_seg - 1)), ("mp", mp, n_mp, steps_mp)
    ):
        for by in steps:
            pl.semaphore_signal(
                barrier, inc=1, device_id={axis: lax.rem(index + by, count)}, device_id_type=MESH
            )
    own = width // n_mp
    w_rows = pl.ds(pl.multiple_of(mp * own, own), own) if relay else pl.ds(0, width)
    w_copy = pltpu.make_async_copy(w_any, w_ref.at[w_rows], local_sem.at[0])
    x_copy = pltpu.make_async_copy(x_any, cur, local_sem.at[1])
    cot_copy = pltpu.make_async_copy(cot_any, up, local_sem.at[2])
    k_copy = pltpu.make_async_copy(k_any, k_bf, local_sem.at[3])
    w_copy.start()
    k_copy.start()

    @pl.when(seg == 0)
    def _():
        x_copy.start()

    @pl.when(seg == n_seg - 1)
    def _():
        cot_copy.start()

    pl.semaphore_wait(barrier, 2 + len(steps_mp))

    row, column = lax.div(mp, 2), lax.rem(mp, 2)
    n_row = n_mp // 2

    def block_copy(block, way):
        rows = pl.ds(pl.multiple_of(block * own, own), own)
        target = (mp + 2, mp - 2, mp + 1 - 2 * column)[way]
        return pltpu.make_async_remote_copy(
            src_ref=w_ref.at[rows], dst_ref=w_ref.at[rows],
            send_sem=w_send.at[way, block], recv_sem=w_recv.at[block],
            device_id={"mp": target}, device_id_type=MESH,
        )

    def each_block(distance, act_on, arrive):
        if distance == 0:
            pl.when(row < n_row - 1)(lambda: act_on(mp, 0))
            pl.when(row > 0)(lambda: act_on(mp, 1))
            act_on(mp, 2)
            return
        low, high = mp - 2 * distance, mp + 2 * distance

        @pl.when(row >= distance)
        def _():
            arrive(low)
            pl.when(row < n_row - 1)(lambda: act_on(low, 0))
            act_on(low, 2)

        @pl.when(row + distance < n_row)
        def _():
            arrive(high)
            pl.when(row > 0)(lambda: act_on(high, 1))
            act_on(high, 2)

    def pass_on(distance):
        each_block(
            distance,
            lambda block, way: block_copy(block, way).start(),
            lambda block: block_copy(block, 0).wait_recv(),
        )

    def passed():
        for distance in range(n_row):
            each_block(
                distance,
                lambda block, way: block_copy(block, way).wait_send(),
                lambda block: None,
            )

    def gather_rest(first):
        if relay:
            for distance in range(first, n_row):
                pass_on(distance)
            for index in range(n_row):
                block_copy(index * 2 + 1 - column, 2).wait_recv()

    def kg_copy(target, sender):
        start = 384 * lax.div(target, 2) + 128 * lax.rem(target, 2)
        window = pl.ds(pl.multiple_of(start, LANES), 2 * LANES)
        return pltpu.make_async_remote_copy(
            src_ref=kg_ref.at[:, window], dst_ref=kg_land.at[sender],
            send_sem=kg_send.at[target], recv_sem=kg_recv.at[sender],
            device_id={"mp": target}, device_id_type=MESH,
        )

    w_copy.wait()
    if relay:

        @pl.when(seg != 1)
        def _():
            pass_on(0)

    k_copy.wait()
    k_ref[...] = k_bf[...].astype(F32)
    kg_ref[...] = jnp.zeros(kg_ref.shape, F32)

    def halo_copy(pad_ref, first, to_right):
        rows_from = pl.ds(frames, PAD) if to_right else pl.ds(PAD, PAD)
        rows_to = pl.ds(0, PAD) if to_right else pl.ds(frames + PAD, PAD)
        target = lax.rem(mp + (1 if to_right else n_mp - 1), n_mp)
        slot = first + (0 if to_right else 1)
        return pltpu.make_async_remote_copy(
            src_ref=pad_ref.at[rows_from], dst_ref=pad_ref.at[rows_to],
            send_sem=halo_send.at[slot], recv_sem=halo_recv.at[slot],
            device_id={"mp": target}, device_id_type=MESH,
        )

    def halo_start(pad_ref, first):
        @pl.when(mp < n_mp - 1)
        def _():
            halo_copy(pad_ref, first, True).start()

        @pl.when(mp > 0)
        def _():
            halo_copy(pad_ref, first, False).start()

    def halo_wait(pad_ref, first):
        @pl.when(mp > 0)
        def _():
            halo_copy(pad_ref, first, True).wait_recv()

        @pl.when(mp < n_mp - 1)
        def _():
            halo_copy(pad_ref, first, False).wait_recv()

    def halo_sent(pad_ref, first):
        @pl.when(mp < n_mp - 1)
        def _():
            halo_copy(pad_ref, first, True).wait_send()

        @pl.when(mp > 0)
        def _():
            halo_copy(pad_ref, first, False).wait_send()

    def halo_clear(pad_ref):
        @pl.when(mp == 0)
        def _():
            pad_ref[0:PAD, :] = jnp.zeros((PAD, width), BF)

        @pl.when(mp == n_mp - 1)
        def _():
            pad_ref[frames + PAD : frames + 2 * PAD, :] = jnp.zeros((PAD, width), BF)

    def in_copy(tile):
        columns = pl.ds(tile * WIDE, WIDE)
        return pltpu.make_async_remote_copy(
            src_ref=out_ref.at[:, columns], dst_ref=cur.at[:, columns],
            send_sem=in_send.at[tile], recv_sem=in_recv.at[tile],
            device_id={"segment": lax.rem(seg + 1, n_seg)}, device_id_type=MESH,
        )

    def up_copy(block):
        rows = pl.ds(block * ROWS, ROWS)
        return pltpu.make_async_remote_copy(
            src_ref=gin_ref.at[rows], dst_ref=up.at[rows],
            send_sem=up_send.at[block], recv_sem=up_recv.at[block],
            device_id={"segment": lax.rem(seg + n_seg - 1, n_seg)}, device_id_type=MESH,
        )

    def mask_rows(start, count):
        position = mp * frames + start + lax.broadcasted_iota(jnp.int32, (count, LANES), 0)
        return (position < vl_ref[0]).astype(F32)

    def back_product():
        for tile in range(tiles):
            columns = slice(tile * WIDE, (tile + 1) * WIDE)
            gs[:, columns] = lax.dot_general(
                up[...], w_ref[columns, :], (((1,), (1,)), ((), ())), preferred_element_type=F32
            )

    halo_clear(pm)
    halo_clear(pg)

    @pl.when(seg == n_seg - 1)
    def _():
        gather_rest(1)
        cot_copy.wait()
        back_product()

    @pl.when(seg == 0)
    def _():
        x_copy.wait()

    @pl.when(seg == 1)
    def _():
        if relay:
            pl.semaphore_wait(turn_sem, 1)
            pass_on(0)

    @pl.when((seg > 1) & (seg < n_seg - 1))
    def _():
        gather_rest(1)

    @pl.when(seg > 0)
    def _():
        for tile in range(tiles):
            in_copy(tile).wait_recv()

    def norm_rows(block):
        start = pl.multiple_of(block * ROWS, ROWS)
        rows = pl.ds(start, ROWS)
        values = cur[rows, :].astype(F32)
        center = values - jnp.mean(values, axis=-1, keepdims=True)
        inverse = lax.rsqrt(jnp.mean(center * center, axis=-1, keepdims=True) + EPSILON)
        normed = center * inverse
        norm[rows, :] = normed
        inv[rows, :] = jnp.broadcast_to(inverse, (ROWS, LANES))
        pm[pl.ds(pl.multiple_of(PAD + start, ROWS), ROWS), :] = (
            normed * mask_rows(start, ROWS)[:, :1]
        ).astype(BF)

    norm_rows(0)
    norm_rows(blocks - 1)
    halo_start(pm, 0)

    @pl.loop(1, blocks - 1)
    def _(block):
        norm_rows(block)

    if relay:

        @pl.when(seg < 2)
        def _():
            pass_on(1)

    halo_wait(pm, 0)

    def shifted(padded):
        total = padded.shape[0]
        return [padded if r == 0 else pltpu.roll(padded, total - r, 0) for r in range(8)]

    def tap_sum(padded, columns, forward):
        total = padded.shape[0]
        running = jnp.zeros((frames, LANES), F32)
        for r in range(8):
            moved = padded if r == 0 else pltpu.roll(padded, total - r, 0)
            for base in range(0, 2 * PAD, 8):
                offset = base + r
                if 1 <= offset <= taps:
                    tap = offset - 1 if forward else taps - offset
                    running = running + k_ref[tap : tap + 1, columns] * moved[base : base + frames]
        return running

    @pl.loop(0, chunks)
    def _(chunk):
        columns = pl.ds(pl.multiple_of(chunk * LANES, LANES), LANES)
        conv = tap_sum(pm[:, columns].astype(F32), columns, True)
        gate = jax.nn.sigmoid(conv)
        act[:, columns] = (conv * gate).astype(BF)
        slope[:, columns] = gate * (1.0 + conv * (1.0 - gate))

    if relay:

        @pl.when(seg < 2)
        def _():
            pass_on(2)

        @pl.when(seg == 0)
        def _():
            pl.semaphore_signal(
                turn_sem, inc=1, device_id={"segment": seg + 1}, device_id_type=MESH
            )

        @pl.when(seg < 2)
        def _():
            gather_rest(3)

    for tile in range(tiles):
        columns = slice(tile * WIDE, (tile + 1) * WIDE)
        product = jnp.dot(act[...], w_ref[:, columns], preferred_element_type=F32)
        out_ref[:, columns] = (cur[:, columns].astype(F32) + product).astype(BF)

        @pl.when(seg < n_seg - 1)
        def _():
            in_copy(tile).start()

    @pl.when(seg < n_seg - 1)
    def _():
        for block in range(blocks):
            up_copy(block).wait_recv()
        back_product()

    def grad_rows(block):
        start = pl.multiple_of(block * ROWS, ROWS)
        rows = pl.ds(start, ROWS)
        pg[pl.ds(pl.multiple_of(PAD + start, ROWS), ROWS), :] = (
            gs[rows, :] * slope[rows, :]
        ).astype(BF)

    grad_rows(0)
    grad_rows(blocks - 1)
    halo_start(pg, 2)

    @pl.loop(1, blocks - 1)
    def _(block):
        grad_rows(block)

    kg_start = 384 * row + 128 * column
    kg_window = pl.ds(pl.multiple_of(kg_start, LANES), 2 * LANES)

    def tap_grads():
        @pl.loop(0, chunks)
        def _(chunk):
            columns = pl.ds(pl.multiple_of(chunk * LANES, LANES), LANES)
            padded = pm[:, columns].astype(F32)
            grad = pg[PAD : PAD + frames, columns].astype(F32)
            total = padded.shape[0]
            for r in range(8):
                moved = padded if r == 0 else pltpu.roll(padded, total - r, 0)
                for base in range(0, 2 * PAD, 8):
                    tap = base + r - 1
                    if 0 <= tap < taps:
                        kg_ref[tap : tap + 1, columns] = jnp.sum(
                            grad * moved[base : base + frames], axis=0, keepdims=True
                        )

        if relay:
            for by in range(1, n_mp):
                kg_copy(lax.rem(mp + by, n_mp), mp).start()

    @pl.when(seg == 0)
    def _():
        tap_grads()

    halo_wait(pg, 2)

    @pl.loop(0, chunks)
    def _(chunk):
        columns = pl.ds(pl.multiple_of(chunk * LANES, LANES), LANES)
        gs[:, columns] = tap_sum(pg[:, columns].astype(F32), columns, False) * mask_rows(0, frames)

    @pl.loop(0, blocks)
    def _(block):
        rows = pl.ds(pl.multiple_of(block * ROWS, ROWS), ROWS)
        masked = gs[rows, :]
        normed = norm[rows, :]
        first = jnp.mean(masked, axis=-1, keepdims=True)
        second = jnp.mean(masked * normed, axis=-1, keepdims=True)
        grad = inv[rows, :][:, :1] * (masked - first - normed * second)
        gin_ref[rows, :] = (up[rows, :].astype(F32) + grad).astype(BF)

        @pl.when(seg > 0)
        def _():
            up_copy(block).start()

    @pl.when(seg > 0)
    def _():
        tap_grads()

    if relay:
        total = kg_ref[:, kg_window]
        for by in range(1, n_mp):
            sender = lax.rem(mp + n_mp - by, n_mp)
            kg_copy(mp, sender).wait_recv()
            total = total + kg_land[sender]
        scale = (frames * n_mp) ** (-0.5)
        even, odd = total[:taps, :own], total[:taps, 2 * LANES - own :]
        kg_out[0] = jnp.where(column == 0, even, odd) * scale
        for by in range(1, n_mp):
            kg_copy(lax.rem(mp + by, n_mp), mp).wait_send()
        passed()
    else:
        kg_out[0] = kg_ref[:taps, :]

    halo_sent(pm, 0)
    halo_sent(pg, 2)

    @pl.when(seg < n_seg - 1)
    def _():
        for tile in range(tiles):
            in_copy(tile).wait_send()

    @pl.when(seg > 0)
    def _():
        for block in range(blocks):
            up_copy(block).wait_send()


def on_device(frames_in, section_weights, conv_kernels, valid_length, out_cotangent):
    frames, width = frames_in.shape
    taps = conv_kernels.shape[1]
    n_mp = lax.axis_size("mp")
    own = width // n_mp
    relay = own == 192 and n_mp == 8
    weight = section_weights[0]
    if not relay:
        weight = lax.all_gather(weight, "mp", axis=0, tiled=True)
    vmem = pl.BlockSpec(memory_space=pltpu.VMEM)
    smem = pl.BlockSpec(memory_space=pltpu.SMEM)
    whole = pl.BlockSpec(memory_space=pl.ANY)
    padded = (frames + 2 * PAD, width)
    tap_rows = -(-taps // 8) * 8
    dma = pltpu.SemaphoreType.DMA
    out, gin, grad = pl.pallas_call(
        functools.partial(cascade, relay),
        out_shape=(
            jax.ShapeDtypeStruct((1, frames, width), BF),
            jax.ShapeDtypeStruct((1, frames, width), BF),
            jax.ShapeDtypeStruct((1, taps, own if relay else width), F32),
        ),
        in_specs=[whole, whole, whole, smem, whole],
        out_specs=(vmem, vmem, vmem),
        scratch_shapes=[
            pltpu.VMEM((frames, width), BF),
            pltpu.VMEM((frames, width), BF),
            pltpu.VMEM((frames, width), F32),
            pltpu.VMEM((frames, LANES), F32),
            pltpu.VMEM(padded, BF),
            pltpu.VMEM(padded, BF),
            pltpu.VMEM((frames, width), BF),
            pltpu.VMEM((frames, width), F32),
            pltpu.VMEM((frames, width), F32),
            pltpu.VMEM((width, width), BF),
            pltpu.VMEM((taps, width), BF),
            pltpu.VMEM((taps, width), F32),
            pltpu.VMEM((tap_rows, width), F32),
            pltpu.VMEM((n_mp if relay else 1, tap_rows, 2 * LANES), F32),
            dma((4,)), dma((4,)),
            dma((width // WIDE,)), dma((width // WIDE,)),
            dma((frames // ROWS,)), dma((frames // ROWS,)),
            dma((4,)),
            dma((3, n_mp)), dma((n_mp,)), dma((n_mp,)), dma((n_mp,)),
            pltpu.SemaphoreType.REGULAR,
        ],
        compiler_params=pltpu.CompilerParams(
            collective_id=0, has_side_effects=True, vmem_limit_bytes=60 * 2**20
        ),
    )(frames_in, weight, conv_kernels[0], valid_length, out_cotangent)
    if not relay:
        grad = lax.psum_scatter(grad, "mp", scatter_dimension=2, tiled=True)
        grad = grad * (frames * n_mp) ** (-0.5)
    return (out, gin, grad)


def solution(mesh):
    in_specs = (
        P("mp", None),
        P("segment", "mp", None),
        P("segment", None, None),
        P(),
        P("mp", None),
    )
    out_specs = (P("segment", "mp", None), P("segment", "mp", None), P("segment", None, "mp"))
    return jax.shard_map(
        on_device, mesh=mesh, in_specs=in_specs, out_specs=out_specs, check_vma=False
    )
```

```python
import functools

import jax
import jax.numpy as jnp
from jax import lax
from jax.experimental import pallas as pl
from jax.experimental.pallas import tpu as pltpu
from jax.sharding import PartitionSpec as P

EPSILON = 1e-05
PAD = 16
LANES = 128
ROWS = 16
WIDE = 256
MESH = pl.DeviceIdType.MESH
BF = jnp.bfloat16
F32 = jnp.float32


def cascade(
    relay, x_any, w_any, k_any, vl_ref, cot_any,
    out_whole, gin_whole, kg_out,
    cur, up, norm, inv, pm, pg, act, slope, gs, w_ref, k_bf, k_ref, kg_ref, kg_land,
    halo_send, halo_recv, in_send, in_recv, up_send, up_recv,
    local_sem, w_send, w_recv, end_send, end_recv, kg_send, kg_recv, turn_sem,
):
    out_ref, gin_ref = out_whole.at[0], gin_whole.at[0]
    frames, width = x_any.shape
    taps = k_ref.shape[0]
    seg, mp = lax.axis_index("segment"), lax.axis_index("mp")
    n_seg, n_mp = lax.axis_size("segment"), lax.axis_size("mp")
    chunks = width // LANES
    blocks = frames // ROWS
    tiles = width // WIDE

    barrier = pltpu.get_barrier_semaphore()
    steps_mp = range(1, n_mp) if relay else (1, n_mp - 1)
    for axis, index, count, steps in (
        ("segment", seg, n_seg, (1, n_seg - 1)), ("mp", mp, n_mp, steps_mp)
    ):
        for by in steps:
            pl.semaphore_signal(
                barrier, inc=1, device_id={axis: lax.rem(index + by, count)}, device_id_type=MESH
            )
    own = width // n_mp
    w_rows = pl.ds(pl.multiple_of(mp * own, own), own) if relay else pl.ds(0, width)
    w_copy = pltpu.make_async_copy(w_any, w_ref.at[w_rows], local_sem.at[0])
    x_copy = pltpu.make_async_copy(x_any, cur, local_sem.at[1])
    cot_copy = pltpu.make_async_copy(cot_any, up, local_sem.at[2])
    k_copy = pltpu.make_async_copy(k_any, k_bf, local_sem.at[3])
    w_copy.start()
    k_copy.start()

    @pl.when(seg == 0)
    def _():
        x_copy.start()

    @pl.when(seg == n_seg - 1)
    def _():
        cot_copy.start()

    pl.semaphore_wait(barrier, 2 + len(steps_mp))

    row, column = lax.div(mp, 2), lax.rem(mp, 2)
    n_row = n_mp // 2

    half = own // 2

    def block_copy(block, way, count=own):
        rows = pl.ds(pl.multiple_of(block * own, own), count)
        target = (mp + 2, mp - 2, mp + 1 - 2 * column)[way]
        return pltpu.make_async_remote_copy(
            src_ref=w_ref.at[rows], dst_ref=w_ref.at[rows],
            send_sem=w_send.at[way, block], recv_sem=w_recv.at[block],
            device_id={"mp": target}, device_id_type=MESH,
        )

    def end_copy(way):
        block = (0 if way == 0 else n_mp - 2) + 1 - column
        rows = pl.ds(pl.multiple_of(block * own + half, half), half)
        return pltpu.make_async_remote_copy(
            src_ref=w_ref.at[rows], dst_ref=w_ref.at[rows],
            send_sem=end_send.at[way], recv_sem=end_recv.at[way],
            device_id={"mp": mp + 2 if way == 0 else mp - 2}, device_id_type=MESH,
        )

    def each_block(distance, act_on, arrive):
        if distance == 0:
            pl.when(row < n_row - 1)(lambda: act_on(mp, 0))
            pl.when(row > 0)(lambda: act_on(mp, 1))
            act_on(mp, 2)
            return
        low, high = mp - 2 * distance, mp + 2 * distance

        @pl.when(row >= distance)
        def _():
            arrive(low)
            pl.when(row < n_row - 1)(lambda: act_on(low, 0))
            pl.when(row == distance)(lambda: act_on(low, 2, half))
            pl.when(row > distance)(lambda: act_on(low, 2))

        @pl.when(row + distance < n_row)
        def _():
            arrive(high)
            pl.when(row > 0)(lambda: act_on(high, 1))
            pl.when(row + distance == n_row - 1)(lambda: act_on(high, 2, half))
            pl.when(row + distance < n_row - 1)(lambda: act_on(high, 2))

    def pass_on(distance):
        each_block(
            distance,
            lambda *what: block_copy(*what).start(),
            lambda block: block_copy(block, 0).wait_recv(),
        )
        if distance == 1:
            for way, end in ((0, 0), (1, n_row - 1)):

                @pl.when(row == end)
                def _():
                    block_copy(2 * end + 1 - column, 2).wait_recv()
                    end_copy(way).start()

    def passed():
        for distance in range(n_row):
            each_block(
                distance,
                lambda *what: block_copy(*what).wait_send(),
                lambda block: None,
            )
        pl.when(row < n_row - 1)(lambda: end_copy(0).wait_send())
        pl.when(row > 0)(lambda: end_copy(1).wait_send())

    def gather_rest(first):
        if relay:
            for distance in range(first, n_row):
                pass_on(distance)

            @pl.when(row > 0)
            def _():
                end_copy(0).wait_recv()
                pl.when(row < n_row - 1)(lambda: end_copy(0).start())

            @pl.when(row < n_row - 1)
            def _():
                end_copy(1).wait_recv()
                pl.when(row > 0)(lambda: end_copy(1).start())

            for index in range(n_row):
                block = index * 2 + 1 - column
                if index in (0, n_row - 1):
                    pl.when(row != index)(lambda: block_copy(block, 2, half).wait_recv())
                else:
                    block_copy(block, 2).wait_recv()

    def kg_copy(target, sender):
        start = 384 * lax.div(target, 2) + 128 * lax.rem(target, 2)
        window = pl.ds(pl.multiple_of(start, LANES), 2 * LANES)
        return pltpu.make_async_remote_copy(
            src_ref=kg_ref.at[:, window], dst_ref=kg_land.at[sender],
            send_sem=kg_send.at[target], recv_sem=kg_recv.at[sender],
            device_id={"mp": target}, device_id_type=MESH,
        )

    w_copy.wait()
    if relay:

        @pl.when(seg != 1)
        def _():
            pass_on(0)

    k_copy.wait()
    k_ref[...] = k_bf[...].astype(F32)
    kg_ref[...] = jnp.zeros(kg_ref.shape, F32)

    def halo_copy(pad_ref, first, to_right):
        rows_from = pl.ds(frames, PAD) if to_right else pl.ds(PAD, PAD)
        rows_to = pl.ds(0, PAD) if to_right else pl.ds(frames + PAD, PAD)
        target = lax.rem(mp + (1 if to_right else n_mp - 1), n_mp)
        slot = first + (0 if to_right else 1)
        return pltpu.make_async_remote_copy(
            src_ref=pad_ref.at[rows_from], dst_ref=pad_ref.at[rows_to],
            send_sem=halo_send.at[slot], recv_sem=halo_recv.at[slot],
            device_id={"mp": target}, device_id_type=MESH,
        )

    def halo_start(pad_ref, first):
        @pl.when(mp < n_mp - 1)
        def _():
            halo_copy(pad_ref, first, True).start()

        @pl.when(mp > 0)
        def _():
            halo_copy(pad_ref, first, False).start()

    def halo_wait(pad_ref, first):
        @pl.when(mp > 0)
        def _():
            halo_copy(pad_ref, first, True).wait_recv()

        @pl.when(mp < n_mp - 1)
        def _():
            halo_copy(pad_ref, first, False).wait_recv()

    def halo_sent(pad_ref, first):
        @pl.when(mp < n_mp - 1)
        def _():
            halo_copy(pad_ref, first, True).wait_send()

        @pl.when(mp > 0)
        def _():
            halo_copy(pad_ref, first, False).wait_send()

    def halo_clear(pad_ref):
        @pl.when(mp == 0)
        def _():
            pad_ref[0:PAD, :] = jnp.zeros((PAD, width), BF)

        @pl.when(mp == n_mp - 1)
        def _():
            pad_ref[frames + PAD : frames + 2 * PAD, :] = jnp.zeros((PAD, width), BF)

    def in_copy(tile):
        columns = pl.ds(tile * WIDE, WIDE)
        return pltpu.make_async_remote_copy(
            src_ref=out_ref.at[:, columns], dst_ref=cur.at[:, columns],
            send_sem=in_send.at[tile], recv_sem=in_recv.at[tile],
            device_id={"segment": lax.rem(seg + 1, n_seg)}, device_id_type=MESH,
        )

    def up_copy(block):
        rows = pl.ds(block * ROWS, ROWS)
        return pltpu.make_async_remote_copy(
            src_ref=gin_ref.at[rows], dst_ref=up.at[rows],
            send_sem=up_send.at[block], recv_sem=up_recv.at[block],
            device_id={"segment": lax.rem(seg + n_seg - 1, n_seg)}, device_id_type=MESH,
        )

    def mask_rows(start, count):
        position = mp * frames + start + lax.broadcasted_iota(jnp.int32, (count, LANES), 0)
        return (position < vl_ref[0]).astype(F32)

    def back_product():
        for tile in range(tiles):
            columns = slice(tile * WIDE, (tile + 1) * WIDE)
            gs[:, columns] = lax.dot_general(
                up[...], w_ref[columns, :], (((1,), (1,)), ((), ())), preferred_element_type=F32
            )

    halo_clear(pm)
    halo_clear(pg)

    @pl.when(seg == n_seg - 1)
    def _():
        gather_rest(1)
        cot_copy.wait()
        back_product()

    @pl.when(seg == 0)
    def _():
        x_copy.wait()

    @pl.when(seg == 1)
    def _():
        if relay:
            pl.semaphore_wait(turn_sem, 1)
            pass_on(0)

    @pl.when((seg > 1) & (seg < n_seg - 1))
    def _():
        gather_rest(1)

    @pl.when(seg > 0)
    def _():
        for tile in range(tiles):
            in_copy(tile).wait_recv()

    def norm_rows(block):
        start = pl.multiple_of(block * ROWS, ROWS)
        rows = pl.ds(start, ROWS)
        values = cur[rows, :].astype(F32)
        center = values - jnp.mean(values, axis=-1, keepdims=True)
        inverse = lax.rsqrt(jnp.mean(center * center, axis=-1, keepdims=True) + EPSILON)
        normed = center * inverse
        norm[rows, :] = normed
        inv[rows, :] = jnp.broadcast_to(inverse, (ROWS, LANES))
        pm[pl.ds(pl.multiple_of(PAD + start, ROWS), ROWS), :] = (
            normed * mask_rows(start, ROWS)[:, :1]
        ).astype(BF)

    norm_rows(0)
    norm_rows(blocks - 1)
    halo_start(pm, 0)

    @pl.loop(1, blocks - 1)
    def _(block):
        norm_rows(block)

    if relay:

        @pl.when(seg < 2)
        def _():
            pass_on(1)

    halo_wait(pm, 0)

    def shifted(padded):
        total = padded.shape[0]
        return [padded if r == 0 else pltpu.roll(padded, total - r, 0) for r in range(8)]

    def tap_sum(padded, columns, forward):
        total = padded.shape[0]
        running = jnp.zeros((frames, LANES), F32)
        for r in range(8):
            moved = padded if r == 0 else pltpu.roll(padded, total - r, 0)
            for base in range(0, 2 * PAD, 8):
                offset = base + r
                if 1 <= offset <= taps:
                    tap = offset - 1 if forward else taps - offset
                    running = running + k_ref[tap : tap + 1, columns] * moved[base : base + frames]
        return running

    @pl.loop(0, chunks)
    def _(chunk):
        columns = pl.ds(pl.multiple_of(chunk * LANES, LANES), LANES)
        conv = tap_sum(pm[:, columns].astype(F32), columns, True)
        gate = jax.nn.sigmoid(conv)
        act[:, columns] = (conv * gate).astype(BF)
        slope[:, columns] = gate * (1.0 + conv * (1.0 - gate))

    if relay:

        @pl.when(seg < 2)
        def _():
            pass_on(2)

        @pl.when(seg == 0)
        def _():
            pl.semaphore_signal(
                turn_sem, inc=1, device_id={"segment": seg + 1}, device_id_type=MESH
            )

        @pl.when(seg < 2)
        def _():
            gather_rest(3)

    for tile in range(tiles):
        columns = slice(tile * WIDE, (tile + 1) * WIDE)
        product = jnp.dot(act[...], w_ref[:, columns], preferred_element_type=F32)
        out_ref[:, columns] = (cur[:, columns].astype(F32) + product).astype(BF)

        @pl.when(seg < n_seg - 1)
        def _():
            in_copy(tile).start()

    @pl.when(seg < n_seg - 1)
    def _():
        for block in range(blocks):
            up_copy(block).wait_recv()
        back_product()

    def grad_rows(block):
        start = pl.multiple_of(block * ROWS, ROWS)
        rows = pl.ds(start, ROWS)
        pg[pl.ds(pl.multiple_of(PAD + start, ROWS), ROWS), :] = (
            gs[rows, :] * slope[rows, :]
        ).astype(BF)

    grad_rows(0)
    grad_rows(blocks - 1)
    halo_start(pg, 2)

    @pl.loop(1, blocks - 1)
    def _(block):
        grad_rows(block)

    kg_start = 384 * row + 128 * column
    kg_window = pl.ds(pl.multiple_of(kg_start, LANES), 2 * LANES)

    def tap_grads():
        @pl.loop(0, chunks)
        def _(chunk):
            columns = pl.ds(pl.multiple_of(chunk * LANES, LANES), LANES)
            padded = pm[:, columns].astype(F32)
            grad = pg[PAD : PAD + frames, columns].astype(F32)
            total = padded.shape[0]
            for r in range(8):
                moved = padded if r == 0 else pltpu.roll(padded, total - r, 0)
                for base in range(0, 2 * PAD, 8):
                    tap = base + r - 1
                    if 0 <= tap < taps:
                        kg_ref[tap : tap + 1, columns] = jnp.sum(
                            grad * moved[base : base + frames], axis=0, keepdims=True
                        )

        if relay:
            for by in range(1, n_mp):
                kg_copy(lax.rem(mp + by, n_mp), mp).start()

    @pl.when(seg == 0)
    def _():
        tap_grads()

    halo_wait(pg, 2)

    @pl.loop(0, chunks)
    def _(chunk):
        columns = pl.ds(pl.multiple_of(chunk * LANES, LANES), LANES)
        gs[:, columns] = tap_sum(pg[:, columns].astype(F32), columns, False) * mask_rows(0, frames)

    @pl.loop(0, blocks)
    def _(block):
        rows = pl.ds(pl.multiple_of(block * ROWS, ROWS), ROWS)
        masked = gs[rows, :]
        normed = norm[rows, :]
        first = jnp.mean(masked, axis=-1, keepdims=True)
        second = jnp.mean(masked * normed, axis=-1, keepdims=True)
        grad = inv[rows, :][:, :1] * (masked - first - normed * second)
        gin_ref[rows, :] = (up[rows, :].astype(F32) + grad).astype(BF)

        @pl.when(seg > 0)
        def _():
            up_copy(block).start()

    @pl.when(seg > 0)
    def _():
        tap_grads()

    if relay:
        total = kg_ref[:, kg_window]
        for by in range(1, n_mp):
            sender = lax.rem(mp + n_mp - by, n_mp)
            kg_copy(mp, sender).wait_recv()
            total = total + kg_land[sender]
        scale = (frames * n_mp) ** (-0.5)
        even, odd = total[:taps, :own], total[:taps, 2 * LANES - own :]
        kg_out[0] = jnp.where(column == 0, even, odd) * scale
        for by in range(1, n_mp):
            kg_copy(lax.rem(mp + by, n_mp), mp).wait_send()
        passed()
    else:
        kg_out[0] = kg_ref[:taps, :]

    halo_sent(pm, 0)
    halo_sent(pg, 2)

    @pl.when(seg < n_seg - 1)
    def _():
        for tile in range(tiles):
            in_copy(tile).wait_send()

    @pl.when(seg > 0)
    def _():
        for block in range(blocks):
            up_copy(block).wait_send()


def on_device(frames_in, section_weights, conv_kernels, valid_length, out_cotangent):
    frames, width = frames_in.shape
    taps = conv_kernels.shape[1]
    n_mp = lax.axis_size("mp")
    own = width // n_mp
    relay = own == 192 and n_mp == 8
    weight = section_weights[0]
    if not relay:
        weight = lax.all_gather(weight, "mp", axis=0, tiled=True)
    vmem = pl.BlockSpec(memory_space=pltpu.VMEM)
    smem = pl.BlockSpec(memory_space=pltpu.SMEM)
    whole = pl.BlockSpec(memory_space=pl.ANY)
    padded = (frames + 2 * PAD, width)
    tap_rows = -(-taps // 8) * 8
    dma = pltpu.SemaphoreType.DMA
    out, gin, grad = pl.pallas_call(
        functools.partial(cascade, relay),
        out_shape=(
            jax.ShapeDtypeStruct((1, frames, width), BF),
            jax.ShapeDtypeStruct((1, frames, width), BF),
            jax.ShapeDtypeStruct((1, taps, own if relay else width), F32),
        ),
        in_specs=[whole, whole, whole, smem, whole],
        out_specs=(vmem, vmem, vmem),
        scratch_shapes=[
            pltpu.VMEM((frames, width), BF),
            pltpu.VMEM((frames, width), BF),
            pltpu.VMEM((frames, width), F32),
            pltpu.VMEM((frames, LANES), F32),
            pltpu.VMEM(padded, BF),
            pltpu.VMEM(padded, BF),
            pltpu.VMEM((frames, width), BF),
            pltpu.VMEM((frames, width), F32),
            pltpu.VMEM((frames, width), F32),
            pltpu.VMEM((width, width), BF),
            pltpu.VMEM((taps, width), BF),
            pltpu.VMEM((taps, width), F32),
            pltpu.VMEM((tap_rows, width), F32),
            pltpu.VMEM((n_mp if relay else 1, tap_rows, 2 * LANES), F32),
            dma((4,)), dma((4,)),
            dma((width // WIDE,)), dma((width // WIDE,)),
            dma((frames // ROWS,)), dma((frames // ROWS,)),
            dma((4,)),
            dma((3, n_mp)), dma((n_mp,)), dma((2,)), dma((2,)), dma((n_mp,)), dma((n_mp,)),
            pltpu.SemaphoreType.REGULAR,
        ],
        compiler_params=pltpu.CompilerParams(
            collective_id=0, has_side_effects=True, vmem_limit_bytes=60 * 2**20
        ),
    )(frames_in, weight, conv_kernels[0], valid_length, out_cotangent)
    if not relay:
        grad = lax.psum_scatter(grad, "mp", scatter_dimension=2, tiled=True)
        grad = grad * (frames * n_mp) ** (-0.5)
    return (out, gin, grad)


def solution(mesh):
    in_specs = (
        P("mp", None),
        P("segment", "mp", None),
        P("segment", None, None),
        P(),
        P("mp", None),
    )
    out_specs = (P("segment", "mp", None), P("segment", "mp", None), P("segment", None, "mp"))
    return jax.shard_map(
        on_device, mesh=mesh, in_specs=in_specs, out_specs=out_specs, check_vma=False
    )
```

```python
import functools

import jax
import jax.numpy as jnp
from jax import lax
from jax.experimental import pallas as pl
from jax.experimental.pallas import tpu as pltpu
from jax.sharding import PartitionSpec as P

EPSILON = 1e-05
PAD = 16
LANES = 128
ROWS = 16
WIDE = 256
MESH = pl.DeviceIdType.MESH
BF = jnp.bfloat16
F32 = jnp.float32


def cascade(
    relay, x_any, w_any, k_any, vl_ref, cot_any,
    out_whole, gin_whole, kg_out,
    cur, up, norm, inv, pm, pg, act, slope, gs, out_ref, gin_ref, w_ref, k_bf, k_ref, kg_ref, kg_land,
    halo_send, halo_recv, in_send, in_recv, up_send, up_recv,
    local_sem, w_send, w_recv, end_send, end_recv, kg_send, kg_recv, turn_sem,
):
    frames, width = x_any.shape
    taps = k_ref.shape[0]
    seg, mp = lax.axis_index("segment"), lax.axis_index("mp")
    n_seg, n_mp = lax.axis_size("segment"), lax.axis_size("mp")
    chunks = width // LANES
    blocks = frames // ROWS
    tiles = width // WIDE

    barrier = pltpu.get_barrier_semaphore()
    steps_mp = range(1, n_mp) if relay else (1, n_mp - 1)
    for axis, index, count, steps in (
        ("segment", seg, n_seg, (1, n_seg - 1)), ("mp", mp, n_mp, steps_mp)
    ):
        for by in steps:
            pl.semaphore_signal(
                barrier, inc=1, device_id={axis: lax.rem(index + by, count)}, device_id_type=MESH
            )
    own = width // n_mp
    w_rows = pl.ds(pl.multiple_of(mp * own, own), own) if relay else pl.ds(0, width)
    w_copy = pltpu.make_async_copy(w_any, w_ref.at[w_rows], local_sem.at[0])
    x_copy = pltpu.make_async_copy(x_any, cur, local_sem.at[1])
    cot_copy = pltpu.make_async_copy(cot_any, up, local_sem.at[2])
    k_copy = pltpu.make_async_copy(k_any, k_bf, local_sem.at[3])
    out_copy = pltpu.make_async_copy(out_ref, out_whole.at[0], local_sem.at[4])
    gin_copy = pltpu.make_async_copy(gin_ref, gin_whole.at[0], local_sem.at[5])
    w_copy.start()
    k_copy.start()

    @pl.when(seg == 0)
    def _():
        x_copy.start()

    @pl.when(seg == n_seg - 1)
    def _():
        cot_copy.start()

    pl.semaphore_wait(barrier, 2 + len(steps_mp))

    row, column = lax.div(mp, 2), lax.rem(mp, 2)
    n_row = n_mp // 2

    half = own // 2

    def block_copy(block, way, count=own):
        rows = pl.ds(pl.multiple_of(block * own, own), count)
        target = (mp + 2, mp - 2, mp + 1 - 2 * column)[way]
        return pltpu.make_async_remote_copy(
            src_ref=w_ref.at[rows], dst_ref=w_ref.at[rows],
            send_sem=w_send.at[way, block], recv_sem=w_recv.at[block],
            device_id={"mp": target}, device_id_type=MESH,
        )

    def end_copy(way):
        block = (0 if way == 0 else n_mp - 2) + 1 - column
        rows = pl.ds(pl.multiple_of(block * own + half, half), half)
        return pltpu.make_async_remote_copy(
            src_ref=w_ref.at[rows], dst_ref=w_ref.at[rows],
            send_sem=end_send.at[way], recv_sem=end_recv.at[way],
            device_id={"mp": mp + 2 if way == 0 else mp - 2}, device_id_type=MESH,
        )

    def each_block(distance, act_on, arrive):
        if distance == 0:
            pl.when(row < n_row - 1)(lambda: act_on(mp, 0))
            pl.when(row > 0)(lambda: act_on(mp, 1))
            act_on(mp, 2)
            return
        low, high = mp - 2 * distance, mp + 2 * distance

        @pl.when(row >= distance)
        def _():
            arrive(low)
            pl.when(row < n_row - 1)(lambda: act_on(low, 0))
            pl.when(row == distance)(lambda: act_on(low, 2, half))
            pl.when(row > distance)(lambda: act_on(low, 2))

        @pl.when(row + distance < n_row)
        def _():
            arrive(high)
            pl.when(row > 0)(lambda: act_on(high, 1))
            pl.when(row + distance == n_row - 1)(lambda: act_on(high, 2, half))
            pl.when(row + distance < n_row - 1)(lambda: act_on(high, 2))

    def pass_on(distance):
        each_block(
            distance,
            lambda *what: block_copy(*what).start(),
            lambda block: block_copy(block, 0).wait_recv(),
        )
        if distance == 1:
            for way, end in ((0, 0), (1, n_row - 1)):

                @pl.when(row == end)
                def _():
                    block_copy(2 * end + 1 - column, 2).wait_recv()
                    end_copy(way).start()

    def passed():
        for distance in range(n_row):
            each_block(
                distance,
                lambda *what: block_copy(*what).wait_send(),
                lambda block: None,
            )
        pl.when(row < n_row - 1)(lambda: end_copy(0).wait_send())
        pl.when(row > 0)(lambda: end_copy(1).wait_send())

    def gather_rest(first):
        if relay:
            for distance in range(first, n_row):
                pass_on(distance)

            @pl.when(row > 0)
            def _():
                end_copy(0).wait_recv()
                pl.when(row < n_row - 1)(lambda: end_copy(0).start())

            @pl.when(row < n_row - 1)
            def _():
                end_copy(1).wait_recv()
                pl.when(row > 0)(lambda: end_copy(1).start())

            for index in range(n_row):
                block = index * 2 + 1 - column
                if index in (0, n_row - 1):
                    pl.when(row != index)(lambda: block_copy(block, 2, half).wait_recv())
                else:
                    block_copy(block, 2).wait_recv()

    def kg_copy(target, sender):
        start = 384 * lax.div(target, 2) + 128 * lax.rem(target, 2)
        window = pl.ds(pl.multiple_of(start, LANES), 2 * LANES)
        return pltpu.make_async_remote_copy(
            src_ref=kg_ref.at[:, window], dst_ref=kg_land.at[sender],
            send_sem=kg_send.at[target], recv_sem=kg_recv.at[sender],
            device_id={"mp": target}, device_id_type=MESH,
        )

    w_copy.wait()
    if relay:

        @pl.when(seg != 1)
        def _():
            pass_on(0)

    k_copy.wait()
    k_ref[...] = k_bf[...].astype(F32)
    kg_ref[...] = jnp.zeros(kg_ref.shape, F32)

    def halo_copy(pad_ref, first, to_right):
        rows_from = pl.ds(frames, PAD) if to_right else pl.ds(PAD, PAD)
        rows_to = pl.ds(0, PAD) if to_right else pl.ds(frames + PAD, PAD)
        target = lax.rem(mp + (1 if to_right else n_mp - 1), n_mp)
        slot = first + (0 if to_right else 1)
        return pltpu.make_async_remote_copy(
            src_ref=pad_ref.at[rows_from], dst_ref=pad_ref.at[rows_to],
            send_sem=halo_send.at[slot], recv_sem=halo_recv.at[slot],
            device_id={"mp": target}, device_id_type=MESH,
        )

    def halo_start(pad_ref, first):
        @pl.when(mp < n_mp - 1)
        def _():
            halo_copy(pad_ref, first, True).start()

        @pl.when(mp > 0)
        def _():
            halo_copy(pad_ref, first, False).start()

    def halo_wait(pad_ref, first):
        @pl.when(mp > 0)
        def _():
            halo_copy(pad_ref, first, True).wait_recv()

        @pl.when(mp < n_mp - 1)
        def _():
            halo_copy(pad_ref, first, False).wait_recv()

    def halo_sent(pad_ref, first):
        @pl.when(mp < n_mp - 1)
        def _():
            halo_copy(pad_ref, first, True).wait_send()

        @pl.when(mp > 0)
        def _():
            halo_copy(pad_ref, first, False).wait_send()

    def halo_clear(pad_ref):
        @pl.when(mp == 0)
        def _():
            pad_ref[0:PAD, :] = jnp.zeros((PAD, width), BF)

        @pl.when(mp == n_mp - 1)
        def _():
            pad_ref[frames + PAD : frames + 2 * PAD, :] = jnp.zeros((PAD, width), BF)

    def in_copy(tile):
        columns = pl.ds(tile * WIDE, WIDE)
        return pltpu.make_async_remote_copy(
            src_ref=out_ref.at[:, columns], dst_ref=cur.at[:, columns],
            send_sem=in_send.at[tile], recv_sem=in_recv.at[tile],
            device_id={"segment": lax.rem(seg + 1, n_seg)}, device_id_type=MESH,
        )

    def up_copy(block):
        rows = pl.ds(block * ROWS, ROWS)
        return pltpu.make_async_remote_copy(
            src_ref=gin_ref.at[rows], dst_ref=up.at[rows],
            send_sem=up_send.at[block], recv_sem=up_recv.at[block],
            device_id={"segment": lax.rem(seg + n_seg - 1, n_seg)}, device_id_type=MESH,
        )

    def mask_rows(start, count):
        position = mp * frames + start + lax.broadcasted_iota(jnp.int32, (count, LANES), 0)
        return (position < vl_ref[0]).astype(F32)

    def back_product():
        for tile in range(tiles):
            columns = slice(tile * WIDE, (tile + 1) * WIDE)
            gs[:, columns] = lax.dot_general(
                up[...], w_ref[columns, :], (((1,), (1,)), ((), ())), preferred_element_type=F32
            )

    halo_clear(pm)
    halo_clear(pg)

    @pl.when(seg == n_seg - 1)
    def _():
        gather_rest(1)
        cot_copy.wait()
        back_product()

    @pl.when(seg == 0)
    def _():
        x_copy.wait()

    @pl.when(seg == 1)
    def _():
        if relay:
            pl.semaphore_wait(turn_sem, 1)
            pass_on(0)

    @pl.when((seg > 1) & (seg < n_seg - 1))
    def _():
        gather_rest(1)

    @pl.when(seg > 0)
    def _():
        for tile in range(tiles):
            in_copy(tile).wait_recv()

    def norm_rows(block):
        start = pl.multiple_of(block * ROWS, ROWS)
        rows = pl.ds(start, ROWS)
        values = cur[rows, :].astype(F32)
        center = values - jnp.mean(values, axis=-1, keepdims=True)
        inverse = lax.rsqrt(jnp.mean(center * center, axis=-1, keepdims=True) + EPSILON)
        normed = center * inverse
        norm[rows, :] = normed
        inv[rows, :] = jnp.broadcast_to(inverse, (ROWS, LANES))
        pm[pl.ds(pl.multiple_of(PAD + start, ROWS), ROWS), :] = (
            normed * mask_rows(start, ROWS)[:, :1]
        ).astype(BF)

    norm_rows(0)
    norm_rows(blocks - 1)
    halo_start(pm, 0)

    @pl.loop(1, blocks - 1)
    def _(block):
        norm_rows(block)

    if relay:

        @pl.when(seg < 2)
        def _():
            pass_on(1)

    halo_wait(pm, 0)

    def shifted(padded):
        total = padded.shape[0]
        return [padded if r == 0 else pltpu.roll(padded, total - r, 0) for r in range(8)]

    def tap_sum(padded, columns, forward):
        total = padded.shape[0]
        running = jnp.zeros((frames, LANES), F32)
        for r in range(8):
            moved = padded if r == 0 else pltpu.roll(padded, total - r, 0)
            for base in range(0, 2 * PAD, 8):
                offset = base + r
                if 1 <= offset <= taps:
                    tap = offset - 1 if forward else taps - offset
                    running = running + k_ref[tap : tap + 1, columns] * moved[base : base + frames]
        return running

    @pl.loop(0, chunks)
    def _(chunk):
        columns = pl.ds(pl.multiple_of(chunk * LANES, LANES), LANES)
        conv = tap_sum(pm[:, columns].astype(F32), columns, True)
        gate = jax.nn.sigmoid(conv)
        act[:, columns] = (conv * gate).astype(BF)
        slope[:, columns] = gate * (1.0 + conv * (1.0 - gate))

    if relay:

        @pl.when(seg < 2)
        def _():
            pass_on(2)

        @pl.when(seg == 0)
        def _():
            pl.semaphore_signal(
                turn_sem, inc=1, device_id={"segment": seg + 1}, device_id_type=MESH
            )

        @pl.when(seg < 2)
        def _():
            gather_rest(3)

    for tile in range(tiles):
        columns = slice(tile * WIDE, (tile + 1) * WIDE)
        product = jnp.dot(act[...], w_ref[:, columns], preferred_element_type=F32)
        out_ref[:, columns] = (cur[:, columns].astype(F32) + product).astype(BF)

        @pl.when(seg < n_seg - 1)
        def _():
            in_copy(tile).start()

    out_copy.start()

    @pl.when(seg < n_seg - 1)
    def _():
        for block in range(blocks):
            up_copy(block).wait_recv()
        back_product()

    def grad_rows(block):
        start = pl.multiple_of(block * ROWS, ROWS)
        rows = pl.ds(start, ROWS)
        pg[pl.ds(pl.multiple_of(PAD + start, ROWS), ROWS), :] = (
            gs[rows, :] * slope[rows, :]
        ).astype(BF)

    grad_rows(0)
    grad_rows(blocks - 1)
    halo_start(pg, 2)

    @pl.loop(1, blocks - 1)
    def _(block):
        grad_rows(block)

    kg_start = 384 * row + 128 * column
    kg_window = pl.ds(pl.multiple_of(kg_start, LANES), 2 * LANES)

    def tap_grads():
        @pl.loop(0, chunks)
        def _(chunk):
            columns = pl.ds(pl.multiple_of(chunk * LANES, LANES), LANES)
            padded = pm[:, columns].astype(F32)
            grad = pg[PAD : PAD + frames, columns].astype(F32)
            total = padded.shape[0]
            for r in range(8):
                moved = padded if r == 0 else pltpu.roll(padded, total - r, 0)
                for base in range(0, 2 * PAD, 8):
                    tap = base + r - 1
                    if 0 <= tap < taps:
                        kg_ref[tap : tap + 1, columns] = jnp.sum(
                            grad * moved[base : base + frames], axis=0, keepdims=True
                        )

        if relay:
            for by in range(1, n_mp):
                kg_copy(lax.rem(mp + by, n_mp), mp).start()

    @pl.when(seg == 0)
    def _():
        tap_grads()

    halo_wait(pg, 2)

    @pl.loop(0, chunks)
    def _(chunk):
        columns = pl.ds(pl.multiple_of(chunk * LANES, LANES), LANES)
        gs[:, columns] = tap_sum(pg[:, columns].astype(F32), columns, False) * mask_rows(0, frames)

    @pl.loop(0, blocks)
    def _(block):
        rows = pl.ds(pl.multiple_of(block * ROWS, ROWS), ROWS)
        masked = gs[rows, :]
        normed = norm[rows, :]
        first = jnp.mean(masked, axis=-1, keepdims=True)
        second = jnp.mean(masked * normed, axis=-1, keepdims=True)
        grad = inv[rows, :][:, :1] * (masked - first - normed * second)
        gin_ref[rows, :] = (up[rows, :].astype(F32) + grad).astype(BF)

        @pl.when(seg > 0)
        def _():
            up_copy(block).start()

    gin_copy.start()

    @pl.when(seg > 0)
    def _():
        tap_grads()

    if relay:
        total = kg_ref[:, kg_window]
        for by in range(1, n_mp):
            sender = lax.rem(mp + n_mp - by, n_mp)
            kg_copy(mp, sender).wait_recv()
            total = total + kg_land[sender]
        scale = (frames * n_mp) ** (-0.5)
        even, odd = total[:taps, :own], total[:taps, 2 * LANES - own :]
        kg_out[0] = jnp.where(column == 0, even, odd) * scale
        for by in range(1, n_mp):
            kg_copy(lax.rem(mp + by, n_mp), mp).wait_send()
        passed()
    else:
        kg_out[0] = kg_ref[:taps, :]

    out_copy.wait()
    gin_copy.wait()
    halo_sent(pm, 0)
    halo_sent(pg, 2)

    @pl.when(seg < n_seg - 1)
    def _():
        for tile in range(tiles):
            in_copy(tile).wait_send()

    @pl.when(seg > 0)
    def _():
        for block in range(blocks):
            up_copy(block).wait_send()


def on_device(frames_in, section_weights, conv_kernels, valid_length, out_cotangent):
    frames, width = frames_in.shape
    taps = conv_kernels.shape[1]
    n_mp = lax.axis_size("mp")
    own = width // n_mp
    relay = own == 192 and n_mp == 8
    weight = section_weights[0]
    if not relay:
        weight = lax.all_gather(weight, "mp", axis=0, tiled=True)
    vmem = pl.BlockSpec(memory_space=pltpu.VMEM)
    smem = pl.BlockSpec(memory_space=pltpu.SMEM)
    whole = pl.BlockSpec(memory_space=pl.ANY)
    padded = (frames + 2 * PAD, width)
    tap_rows = -(-taps // 8) * 8
    dma = pltpu.SemaphoreType.DMA
    out, gin, grad = pl.pallas_call(
        functools.partial(cascade, relay),
        out_shape=(
            jax.ShapeDtypeStruct((1, frames, width), BF),
            jax.ShapeDtypeStruct((1, frames, width), BF),
            jax.ShapeDtypeStruct((1, taps, own if relay else width), F32),
        ),
        in_specs=[whole, whole, whole, smem, whole],
        out_specs=(whole, whole, vmem),
        scratch_shapes=[
            pltpu.VMEM((frames, width), BF),
            pltpu.VMEM((frames, width), BF),
            pltpu.VMEM((frames, width), F32),
            pltpu.VMEM((frames, LANES), F32),
            pltpu.VMEM(padded, BF),
            pltpu.VMEM(padded, BF),
            pltpu.VMEM((frames, width), BF),
            pltpu.VMEM((frames, width), F32),
            pltpu.VMEM((frames, width), F32),
            pltpu.VMEM((frames, width), BF),
            pltpu.VMEM((frames, width), BF),
            pltpu.VMEM((width, width), BF),
            pltpu.VMEM((taps, width), BF),
            pltpu.VMEM((taps, width), F32),
            pltpu.VMEM((tap_rows, width), F32),
            pltpu.VMEM((n_mp if relay else 1, tap_rows, 2 * LANES), F32),
            dma((4,)), dma((4,)),
            dma((width // WIDE,)), dma((width // WIDE,)),
            dma((frames // ROWS,)), dma((frames // ROWS,)),
            dma((6,)),
            dma((3, n_mp)), dma((n_mp,)), dma((2,)), dma((2,)), dma((n_mp,)), dma((n_mp,)),
            pltpu.SemaphoreType.REGULAR,
        ],
        compiler_params=pltpu.CompilerParams(
            collective_id=0, has_side_effects=True, vmem_limit_bytes=60 * 2**20
        ),
    )(frames_in, weight, conv_kernels[0], valid_length, out_cotangent)
    if not relay:
        grad = lax.psum_scatter(grad, "mp", scatter_dimension=2, tiled=True)
        grad = grad * (frames * n_mp) ** (-0.5)
    return (out, gin, grad)


def solution(mesh):
    in_specs = (
        P("mp", None),
        P("segment", "mp", None),
        P("segment", None, None),
        P(),
        P("mp", None),
    )
    out_specs = (P("segment", "mp", None), P("segment", "mp", None), P("segment", None, "mp"))
    return jax.shard_map(
        on_device, mesh=mesh, in_specs=in_specs, out_specs=out_specs, check_vma=False
    )
```

```python
import functools

import jax
import jax.numpy as jnp
from jax import lax
from jax.experimental import pallas as pl
from jax.experimental.pallas import tpu as pltpu
from jax.sharding import PartitionSpec as P

EPSILON = 1e-05
PAD = 16
LANES = 128
ROWS = 16
WIDE = 256
MESH = pl.DeviceIdType.MESH
BF = jnp.bfloat16
F32 = jnp.float32


def cascade(
    relay, x_any, w_any, k_any, vl_ref, cot_any,
    out_whole, gin_whole, kg_out,
    cur, up, norm, inv, pm, pg, act, slope, gs, w_ref, k_bf, k_ref, kg_ref, kg_land,
    halo_send, halo_recv, in_send, in_recv, up_send, up_recv,
    local_sem, w_send, w_recv, end_send, end_recv, kg_send, kg_recv, turn_sem,
):
    out_ref, gin_ref = out_whole.at[0], gin_whole.at[0]
    frames, width = x_any.shape
    taps = k_ref.shape[0]
    seg, mp = lax.axis_index("segment"), lax.axis_index("mp")
    n_seg, n_mp = lax.axis_size("segment"), lax.axis_size("mp")
    chunks = width // LANES
    blocks = frames // ROWS
    tiles = width // WIDE

    barrier = pltpu.get_barrier_semaphore()
    steps_mp = range(1, n_mp) if relay else (1, n_mp - 1)
    for axis, index, count, steps in (
        ("segment", seg, n_seg, (1, n_seg - 1)), ("mp", mp, n_mp, steps_mp)
    ):
        for by in steps:
            pl.semaphore_signal(
                barrier, inc=1, device_id={axis: lax.rem(index + by, count)}, device_id_type=MESH
            )
    own = width // n_mp
    w_rows = pl.ds(pl.multiple_of(mp * own, own), own) if relay else pl.ds(0, width)
    w_copy = pltpu.make_async_copy(w_any, w_ref.at[w_rows], local_sem.at[0])
    x_copy = pltpu.make_async_copy(x_any, cur, local_sem.at[1])
    cot_copy = pltpu.make_async_copy(cot_any, up, local_sem.at[2])
    k_copy = pltpu.make_async_copy(k_any, k_bf, local_sem.at[3])
    w_copy.start()
    k_copy.start()

    @pl.when(seg == 0)
    def _():
        x_copy.start()

    @pl.when(seg == n_seg - 1)
    def _():
        cot_copy.start()

    pl.semaphore_wait(barrier, 2 + len(steps_mp))

    row, column = lax.div(mp, 2), lax.rem(mp, 2)
    n_row = n_mp // 2

    half = own // 2

    def block_copy(block, way, count=own):
        rows = pl.ds(pl.multiple_of(block * own, own), count)
        target = (mp + 2, mp - 2, mp + 1 - 2 * column)[way]
        return pltpu.make_async_remote_copy(
            src_ref=w_ref.at[rows], dst_ref=w_ref.at[rows],
            send_sem=w_send.at[way, block], recv_sem=w_recv.at[block],
            device_id={"mp": target}, device_id_type=MESH,
        )

    def end_copy(way):
        block = (0 if way == 0 else n_mp - 2) + 1 - column
        rows = pl.ds(pl.multiple_of(block * own + half, half), half)
        return pltpu.make_async_remote_copy(
            src_ref=w_ref.at[rows], dst_ref=w_ref.at[rows],
            send_sem=end_send.at[way], recv_sem=end_recv.at[way],
            device_id={"mp": mp + 2 if way == 0 else mp - 2}, device_id_type=MESH,
        )

    def each_block(distance, act_on, arrive):
        if distance == 0:
            pl.when(row < n_row - 1)(lambda: act_on(mp, 0))
            pl.when(row > 0)(lambda: act_on(mp, 1))
            act_on(mp, 2)
            return
        low, high = mp - 2 * distance, mp + 2 * distance

        @pl.when(row >= distance)
        def _():
            arrive(low)
            pl.when(row < n_row - 1)(lambda: act_on(low, 0))
            pl.when(row == distance)(lambda: act_on(low, 2, half))
            pl.when(row > distance)(lambda: act_on(low, 2))

        @pl.when(row + distance < n_row)
        def _():
            arrive(high)
            pl.when(row > 0)(lambda: act_on(high, 1))
            pl.when(row + distance == n_row - 1)(lambda: act_on(high, 2, half))
            pl.when(row + distance < n_row - 1)(lambda: act_on(high, 2))

    def pass_on(distance):
        each_block(
            distance,
            lambda *what: block_copy(*what).start(),
            lambda block: block_copy(block, 0).wait_recv(),
        )
        if distance == 1:
            for way, end in ((0, 0), (1, n_row - 1)):

                @pl.when(row == end)
                def _():
                    block_copy(2 * end + 1 - column, 2).wait_recv()
                    end_copy(way).start()

    def passed():
        for distance in range(n_row):
            each_block(
                distance,
                lambda *what: block_copy(*what).wait_send(),
                lambda block: None,
            )
        pl.when(row < n_row - 1)(lambda: end_copy(0).wait_send())
        pl.when(row > 0)(lambda: end_copy(1).wait_send())

    def gather_rest(first):
        if relay:
            for distance in range(first, n_row):
                pass_on(distance)

            @pl.when(row > 0)
            def _():
                end_copy(0).wait_recv()
                pl.when(row < n_row - 1)(lambda: end_copy(0).start())

            @pl.when(row < n_row - 1)
            def _():
                end_copy(1).wait_recv()
                pl.when(row > 0)(lambda: end_copy(1).start())

            for index in range(n_row):
                block = index * 2 + 1 - column
                if index in (0, n_row - 1):
                    pl.when(row != index)(lambda: block_copy(block, 2, half).wait_recv())
                else:
                    block_copy(block, 2).wait_recv()

    def kg_copy(target, sender):
        start = 384 * lax.div(target, 2) + 128 * lax.rem(target, 2)
        window = pl.ds(pl.multiple_of(start, LANES), 2 * LANES)
        return pltpu.make_async_remote_copy(
            src_ref=kg_ref.at[:, window], dst_ref=kg_land.at[sender],
            send_sem=kg_send.at[target], recv_sem=kg_recv.at[sender],
            device_id={"mp": target}, device_id_type=MESH,
        )

    w_copy.wait()
    if relay:

        @pl.when(seg != 1)
        def _():
            pass_on(0)

    k_copy.wait()
    k_ref[...] = k_bf[...].astype(F32)
    kg_ref[...] = jnp.zeros(kg_ref.shape, F32)

    def halo_copy(pad_ref, first, to_right):
        rows_from = pl.ds(frames, PAD) if to_right else pl.ds(PAD, PAD)
        rows_to = pl.ds(0, PAD) if to_right else pl.ds(frames + PAD, PAD)
        target = lax.rem(mp + (1 if to_right else n_mp - 1), n_mp)
        slot = first + (0 if to_right else 1)
        return pltpu.make_async_remote_copy(
            src_ref=pad_ref.at[rows_from], dst_ref=pad_ref.at[rows_to],
            send_sem=halo_send.at[slot], recv_sem=halo_recv.at[slot],
            device_id={"mp": target}, device_id_type=MESH,
        )

    def halo_start(pad_ref, first):
        @pl.when(mp < n_mp - 1)
        def _():
            halo_copy(pad_ref, first, True).start()

        @pl.when(mp > 0)
        def _():
            halo_copy(pad_ref, first, False).start()

    def halo_wait(pad_ref, first):
        @pl.when(mp > 0)
        def _():
            halo_copy(pad_ref, first, True).wait_recv()

        @pl.when(mp < n_mp - 1)
        def _():
            halo_copy(pad_ref, first, False).wait_recv()

    def halo_sent(pad_ref, first):
        @pl.when(mp < n_mp - 1)
        def _():
            halo_copy(pad_ref, first, True).wait_send()

        @pl.when(mp > 0)
        def _():
            halo_copy(pad_ref, first, False).wait_send()

    def halo_clear(pad_ref):
        @pl.when(mp == 0)
        def _():
            pad_ref[0:PAD, :] = jnp.zeros((PAD, width), BF)

        @pl.when(mp == n_mp - 1)
        def _():
            pad_ref[frames + PAD : frames + 2 * PAD, :] = jnp.zeros((PAD, width), BF)

    def in_copy(tile):
        columns = pl.ds(tile * WIDE, WIDE)
        return pltpu.make_async_remote_copy(
            src_ref=out_ref.at[:, columns], dst_ref=cur.at[:, columns],
            send_sem=in_send.at[tile], recv_sem=in_recv.at[tile],
            device_id={"segment": lax.rem(seg + 1, n_seg)}, device_id_type=MESH,
        )

    def up_copy(block):
        rows = pl.ds(block * ROWS, ROWS)
        return pltpu.make_async_remote_copy(
            src_ref=gin_ref.at[rows], dst_ref=up.at[rows],
            send_sem=up_send.at[block], recv_sem=up_recv.at[block],
            device_id={"segment": lax.rem(seg + n_seg - 1, n_seg)}, device_id_type=MESH,
        )

    def mask_rows(start, count):
        position = mp * frames + start + lax.broadcasted_iota(jnp.int32, (count, LANES), 0)
        return (position < vl_ref[0]).astype(F32)

    def back_product():
        for tile in range(tiles):
            columns = slice(tile * WIDE, (tile + 1) * WIDE)
            gs[:, columns] = lax.dot_general(
                up[...], w_ref[columns, :], (((1,), (1,)), ((), ())), preferred_element_type=F32
            )

    halo_clear(pm)
    halo_clear(pg)

    @pl.when(seg == n_seg - 1)
    def _():
        gather_rest(1)
        cot_copy.wait()
        back_product()

    @pl.when(seg == 0)
    def _():
        x_copy.wait()

    @pl.when(seg == 1)
    def _():
        if relay:
            pl.semaphore_wait(turn_sem, 1)
            pass_on(0)

    @pl.when((seg > 1) & (seg < n_seg - 1))
    def _():
        gather_rest(1)

    @pl.when(seg > 0)
    def _():
        for tile in range(tiles):
            in_copy(tile).wait_recv()

    def norm_rows(block):
        start = pl.multiple_of(block * ROWS, ROWS)
        rows = pl.ds(start, ROWS)
        values = cur[rows, :].astype(F32)
        center = values - jnp.mean(values, axis=-1, keepdims=True)
        inverse = lax.rsqrt(jnp.mean(center * center, axis=-1, keepdims=True) + EPSILON)
        normed = center * inverse
        norm[rows, :] = normed
        inv[rows, :] = jnp.broadcast_to(inverse, (ROWS, LANES))
        pm[pl.ds(pl.multiple_of(PAD + start, ROWS), ROWS), :] = (
            normed * mask_rows(start, ROWS)[:, :1]
        ).astype(BF)

    norm_rows(0)
    norm_rows(blocks - 1)
    halo_start(pm, 0)

    @pl.loop(1, blocks - 1)
    def _(block):
        norm_rows(block)

    if relay:

        @pl.when(seg < 2)
        def _():
            pass_on(1)

        @pl.when(seg == 0)
        def _():
            pl.semaphore_signal(
                turn_sem, inc=1, device_id={"segment": seg + 1}, device_id_type=MESH
            )

    halo_wait(pm, 0)

    def shifted(padded):
        total = padded.shape[0]
        return [padded if r == 0 else pltpu.roll(padded, total - r, 0) for r in range(8)]

    def tap_sum(padded, columns, forward):
        total = padded.shape[0]
        running = jnp.zeros((frames, LANES), F32)
        for r in range(8):
            moved = padded if r == 0 else pltpu.roll(padded, total - r, 0)
            for base in range(0, 2 * PAD, 8):
                offset = base + r
                if 1 <= offset <= taps:
                    tap = offset - 1 if forward else taps - offset
                    running = running + k_ref[tap : tap + 1, columns] * moved[base : base + frames]
        return running

    @pl.loop(0, chunks)
    def _(chunk):
        columns = pl.ds(pl.multiple_of(chunk * LANES, LANES), LANES)
        conv = tap_sum(pm[:, columns].astype(F32), columns, True)
        gate = jax.nn.sigmoid(conv)
        act[:, columns] = (conv * gate).astype(BF)
        slope[:, columns] = gate * (1.0 + conv * (1.0 - gate))

    if relay:

        @pl.when(seg < 2)
        def _():
            pass_on(2)

        @pl.when(seg < 2)
        def _():
            gather_rest(3)

    for tile in range(tiles):
        columns = slice(tile * WIDE, (tile + 1) * WIDE)
        product = jnp.dot(act[...], w_ref[:, columns], preferred_element_type=F32)
        out_ref[:, columns] = (cur[:, columns].astype(F32) + product).astype(BF)

        @pl.when(seg < n_seg - 1)
        def _():
            in_copy(tile).start()

    @pl.when(seg < n_seg - 1)
    def _():
        for block in range(blocks):
            up_copy(block).wait_recv()
        back_product()

    def grad_rows(block):
        start = pl.multiple_of(block * ROWS, ROWS)
        rows = pl.ds(start, ROWS)
        pg[pl.ds(pl.multiple_of(PAD + start, ROWS), ROWS), :] = (
            gs[rows, :] * slope[rows, :]
        ).astype(BF)

    grad_rows(0)
    grad_rows(blocks - 1)
    halo_start(pg, 2)

    @pl.loop(1, blocks - 1)
    def _(block):
        grad_rows(block)

    kg_start = 384 * row + 128 * column
    kg_window = pl.ds(pl.multiple_of(kg_start, LANES), 2 * LANES)

    def tap_grads():
        @pl.loop(0, chunks)
        def _(chunk):
            columns = pl.ds(pl.multiple_of(chunk * LANES, LANES), LANES)
            padded = pm[:, columns].astype(F32)
            grad = pg[PAD : PAD + frames, columns].astype(F32)
            total = padded.shape[0]
            for r in range(8):
                moved = padded if r == 0 else pltpu.roll(padded, total - r, 0)
                for base in range(0, 2 * PAD, 8):
                    tap = base + r - 1
                    if 0 <= tap < taps:
                        kg_ref[tap : tap + 1, columns] = jnp.sum(
                            grad * moved[base : base + frames], axis=0, keepdims=True
                        )

        if relay:
            for by in range(1, n_mp):
                kg_copy(lax.rem(mp + by, n_mp), mp).start()

    @pl.when(seg == 0)
    def _():
        tap_grads()

    halo_wait(pg, 2)

    @pl.loop(0, chunks)
    def _(chunk):
        columns = pl.ds(pl.multiple_of(chunk * LANES, LANES), LANES)
        gs[:, columns] = tap_sum(pg[:, columns].astype(F32), columns, False) * mask_rows(0, frames)

    @pl.loop(0, blocks)
    def _(block):
        rows = pl.ds(pl.multiple_of(block * ROWS, ROWS), ROWS)
        masked = gs[rows, :]
        normed = norm[rows, :]
        first = jnp.mean(masked, axis=-1, keepdims=True)
        second = jnp.mean(masked * normed, axis=-1, keepdims=True)
        grad = inv[rows, :][:, :1] * (masked - first - normed * second)
        gin_ref[rows, :] = (up[rows, :].astype(F32) + grad).astype(BF)

        @pl.when(seg > 0)
        def _():
            up_copy(block).start()

    @pl.when(seg > 0)
    def _():
        tap_grads()

    if relay:
        total = kg_ref[:, kg_window]
        for by in range(1, n_mp):
            sender = lax.rem(mp + n_mp - by, n_mp)
            kg_copy(mp, sender).wait_recv()
            total = total + kg_land[sender]
        scale = (frames * n_mp) ** (-0.5)
        even, odd = total[:taps, :own], total[:taps, 2 * LANES - own :]
        kg_out[0] = jnp.where(column == 0, even, odd) * scale
        for by in range(1, n_mp):
            kg_copy(lax.rem(mp + by, n_mp), mp).wait_send()
        passed()
    else:
        kg_out[0] = kg_ref[:taps, :]

    halo_sent(pm, 0)
    halo_sent(pg, 2)

    @pl.when(seg < n_seg - 1)
    def _():
        for tile in range(tiles):
            in_copy(tile).wait_send()

    @pl.when(seg > 0)
    def _():
        for block in range(blocks):
            up_copy(block).wait_send()


def on_device(frames_in, section_weights, conv_kernels, valid_length, out_cotangent):
    frames, width = frames_in.shape
    taps = conv_kernels.shape[1]
    n_mp = lax.axis_size("mp")
    own = width // n_mp
    relay = own == 192 and n_mp == 8
    weight = section_weights[0]
    if not relay:
        weight = lax.all_gather(weight, "mp", axis=0, tiled=True)
    vmem = pl.BlockSpec(memory_space=pltpu.VMEM)
    smem = pl.BlockSpec(memory_space=pltpu.SMEM)
    whole = pl.BlockSpec(memory_space=pl.ANY)
    padded = (frames + 2 * PAD, width)
    tap_rows = -(-taps // 8) * 8
    dma = pltpu.SemaphoreType.DMA
    out, gin, grad = pl.pallas_call(
        functools.partial(cascade, relay),
        out_shape=(
            jax.ShapeDtypeStruct((1, frames, width), BF),
            jax.ShapeDtypeStruct((1, frames, width), BF),
            jax.ShapeDtypeStruct((1, taps, own if relay else width), F32),
        ),
        in_specs=[whole, whole, whole, smem, whole],
        out_specs=(vmem, vmem, vmem),
        scratch_shapes=[
            pltpu.VMEM((frames, width), BF),
            pltpu.VMEM((frames, width), BF),
            pltpu.VMEM((frames, width), F32),
            pltpu.VMEM((frames, LANES), F32),
            pltpu.VMEM(padded, BF),
            pltpu.VMEM(padded, BF),
            pltpu.VMEM((frames, width), BF),
            pltpu.VMEM((frames, width), F32),
            pltpu.VMEM((frames, width), F32),
            pltpu.VMEM((width, width), BF),
            pltpu.VMEM((taps, width), BF),
            pltpu.VMEM((taps, width), F32),
            pltpu.VMEM((tap_rows, width), F32),
            pltpu.VMEM((n_mp if relay else 1, tap_rows, 2 * LANES), F32),
            dma((4,)), dma((4,)),
            dma((width // WIDE,)), dma((width // WIDE,)),
            dma((frames // ROWS,)), dma((frames // ROWS,)),
            dma((4,)),
            dma((3, n_mp)), dma((n_mp,)), dma((2,)), dma((2,)), dma((n_mp,)), dma((n_mp,)),
            pltpu.SemaphoreType.REGULAR,
        ],
        compiler_params=pltpu.CompilerParams(
            collective_id=0, has_side_effects=True, vmem_limit_bytes=60 * 2**20
        ),
    )(frames_in, weight, conv_kernels[0], valid_length, out_cotangent)
    if not relay:
        grad = lax.psum_scatter(grad, "mp", scatter_dimension=2, tiled=True)
        grad = grad * (frames * n_mp) ** (-0.5)
    return (out, gin, grad)


def solution(mesh):
    in_specs = (
        P("mp", None),
        P("segment", "mp", None),
        P("segment", None, None),
        P(),
        P("mp", None),
    )
    out_specs = (P("segment", "mp", None), P("segment", "mp", None), P("segment", None, "mp"))
    return jax.shard_map(
        on_device, mesh=mesh, in_specs=in_specs, out_specs=out_specs, check_vma=False
    )
```
